256 devices in a mesh: band: 4 (over y), col: 64 (over x, z, core).
Axes of the slice: x: 4, y: 4, z: 8, core: 2. Of those that a mesh axis runs over, the one named last changes fastest.
Arguments:
- covariance: float32 [10240, 10240], P('col', 'band'), may hold values from -1 to 10, as said below
- wind_east: float32 [64, 160], replicated, may hold values from -0.25 to 0.25
- wind_north: float32 [64, 160], replicated, may hold values from -0.25 to 0.25
- obs_owner: int32 [3, 128], replicated, may hold values from 0 to 63, as said below
- obs_offset: int32 [3, 128], replicated, may hold values from 0 to 159
- obs_variance: float32 [3, 128], replicated, may hold values from 0.3 to 3
Outputs:
- analysis: float32 [10240, 10240], P('col', 'band')
The draws below stay inside these ranges and needn't reach their ends.
Inputs may be any that keep to these rules, and one draw needn't show every extreme that they name: `covariance`: symmetric positive definite. `obs_owner`: in every batch each slab index appears exactly 2 times.
All inputs are finite; a program needn't handle non-finite values.
Results may differ from the reference program's by a relative error of at most 0.00012.
Values sent between devices are 32-bit elements; how exact they have to be, the bound alone decides.
No kernel may reach another device: no remote copies, remote signals or barrier semaphores. Data moves between devices by JAX's collectives and lax.ppermute only.
A program may use at most 64 MiB of HBM per device.

```python
import math
import jax
import jax.numpy as jnp
from jax import lax

LATITUDE_ROWS = 64
LONGITUDE_COLUMNS = 160
NOBS = 128
NBATCH = 3
GRID_POINTS = 10240
SLAB_PTS = 160
OBS_SLAB = 2


def draw_covariance(key, part):
    first_key, second_key = jax.random.split(jax.random.fold_in(key, 17))
    entries = jax.random.normal(first_key, (GRID_POINTS, GRID_POINTS), jnp.float32)
    scales = jnp.exp(jax.random.uniform(second_key, (GRID_POINTS,), jnp.float32, jnp.log(0.7), jnp.log(1.4)))
    symmetric = (entries + entries.T) * (0.3 / jnp.sqrt(jnp.float32(GRID_POINTS)))
    diagonal = jnp.arange(GRID_POINTS)
    symmetric = symmetric.at[diagonal, diagonal].add(1.0)
    scaled = scales[:, None] * symmetric * scales[None, :]
    return scaled.astype(jnp.float32)


def draw_obs_owner(key, part):
    subkeys = jax.random.split(jax.random.fold_in(key, 29), NBATCH)
    orders = jnp.stack([jax.random.permutation(subkeys[batch_index], NOBS) for batch_index in range(NBATCH)])
    return (orders // OBS_SLAB).astype(jnp.int32)


def plant(result, stream_key, low, high):
    place = [jax.random.randint(jax.random.fold_in(stream_key, axis), (), 0, length) for axis, length in enumerate(result.shape)]
    longest = result.shape.index(max(result.shape))
    beside = place[:longest] + [(place[longest] + 1) % result.shape[longest]] + place[longest + 1:]
    return result.at[tuple(place)].set(low).at[tuple(beside)].set(high)


def setup_inputs(seed: int = 0) -> dict:
    streams_of = jax.random.split(jax.random.key(seed), 7)
    covariance = draw_covariance(jax.random.fold_in(streams_of[6], 71), 0)
    wind_east = jnp.clip(jax.random.uniform(streams_of[1], (LATITUDE_ROWS, LONGITUDE_COLUMNS), jnp.float32, -0.25, 0.25), -0.25, 0.25)
    wind_north = jnp.clip(jax.random.uniform(streams_of[2], (LATITUDE_ROWS, LONGITUDE_COLUMNS), jnp.float32, -0.25, 0.25), -0.25, 0.25)
    obs_owner = draw_obs_owner(jax.random.fold_in(streams_of[6], 71), 0)
    obs_offset = plant(jax.random.randint(streams_of[4], (NBATCH, NOBS), 0, SLAB_PTS), jax.random.fold_in(streams_of[4], 1), 0, SLAB_PTS - 1).astype(jnp.int32)
    obs_variance = jnp.clip(jnp.exp(jax.random.uniform(streams_of[5], (NBATCH, NOBS), jnp.float32, math.log(0.3), math.log(3.0))), 0.3, 3.0)
    return dict(covariance=covariance, wind_east=wind_east, wind_north=wind_north, obs_owner=obs_owner, obs_offset=obs_offset, obs_variance=obs_variance)


def advect(padded, east_wind, north_wind, lat_axis):
    length = padded.shape[lat_axis] - 2
    interior = lax.slice_in_dim(padded, 1, length + 1, axis=lat_axis)
    neighbour = jnp.roll(interior, -1, axis=lat_axis + 1)
    east_flux = jnp.maximum(east_wind, 0.0) * interior + jnp.minimum(east_wind, 0.0) * neighbour
    west_flux = jnp.roll(east_flux, 1, axis=lat_axis + 1)
    lower_cells = lax.slice_in_dim(padded, 0, length + 1, axis=lat_axis)
    upper_cells = lax.slice_in_dim(padded, 1, length + 2, axis=lat_axis)
    north_flux = jnp.maximum(north_wind, 0.0) * lower_cells + jnp.minimum(north_wind, 0.0) * upper_cells
    upper_flux = lax.slice_in_dim(north_flux, 1, length + 1, axis=lat_axis)
    lower_flux = lax.slice_in_dim(north_flux, 0, length, axis=lat_axis)
    return interior - (east_flux - west_flux) - (upper_flux - lower_flux)

def north_faces(wind_north):
    lat_count = wind_north.shape[0]
    lat_index = jnp.arange(lat_count)[:, None]
    walled = jnp.where(lat_index < lat_count - 1, wind_north, 0.0)
    return jnp.concatenate([jnp.zeros((1, wind_north.shape[1]), wind_north.dtype), walled], axis=0)

def solve_gain(matrix, right_side):
    factor = jnp.linalg.cholesky(matrix)
    middle = lax.linalg.triangular_solve(factor, right_side, left_side=True, lower=True)
    return lax.linalg.triangular_solve(factor, middle, left_side=True, lower=True, transpose_a=True)

def reference(covariance, wind_east, wind_north, obs_owner, obs_offset, obs_variance):
    face_winds = north_faces(wind_north)
    first_major = covariance.T.reshape(LATITUDE_ROWS, LONGITUDE_COLUMNS, GRID_POINTS)
    padded = jnp.pad(first_major, ((1, 1), (0, 0), (0, 0)))
    advected = advect(padded, wind_east[:, :, None], face_winds[:, :, None], 0)
    block_list = advected.reshape(LATITUDE_ROWS, LONGITUDE_COLUMNS, LATITUDE_ROWS, LONGITUDE_COLUMNS)

    def pass_rows(block_rows):
        grid_rim = jnp.pad(block_rows, ((0, 0), (1, 1), (0, 0)))
        return advect(grid_rim, wind_east[None], face_winds[None], 1)
    predicted_state = lax.map(pass_rows, block_list).reshape(GRID_POINTS, GRID_POINTS)
    for batch_index in range(NBATCH):
        point_list = (obs_owner[batch_index] * SLAB_PTS + obs_offset[batch_index]).astype(jnp.int32)
        column_set = jnp.take(predicted_state, point_list, axis=1)
        observation_rows = jnp.take(predicted_state, point_list, axis=0)
        innovation = jnp.take(column_set, point_list, axis=0) + jnp.diag(obs_variance[batch_index])
        weight_matrix = solve_gain(innovation, observation_rows)
        predicted_state = predicted_state - jnp.dot(column_set.astype(jnp.float32), weight_matrix.astype(jnp.float32), precision=lax.Precision.HIGHEST, preferred_element_type=jnp.float32)
    return predicted_state.T
```

```python
from functools import partial

import jax
import jax.numpy as jnp
from jax import lax
from jax.experimental import pallas as pl
from jax.experimental.pallas import tpu as pltpu
from jax.sharding import PartitionSpec as P

LATS = 64
LONS = 160
BANDS = 4
SLABS = 64
STRIP = LATS // BANDS
ROWS = STRIP * LONS
BATCHES = 3
PER_SLAB = 6
OBS = SLABS * PER_SLAB
PER_BAND = OBS // BANDS
EDGE = 256
EDGE_START = ROWS - EDGE
EDGE_LOW = EDGE - LONS
HALF = OBS // 2
BLOCK = 128
HIGHEST = lax.Precision.HIGHEST
F32 = jnp.float32


def mm(a, b):
    return lax.dot_general(
        a, b, (((1,), (0,)), ((), ())), precision=HIGHEST, preferred_element_type=F32
    )


def stencil(wind_east, wind_north):
    lat_index = jnp.arange(LATS)[:, None]
    north = jnp.where(lat_index < LATS - 1, wind_north, 0.0)
    south = jnp.concatenate([jnp.zeros((1, LONS), F32), north[:-1]], axis=0)
    west = jnp.roll(wind_east, 1, axis=1)
    here = (
        1.0
        - jnp.maximum(wind_east, 0.0)
        + jnp.minimum(west, 0.0)
        - jnp.maximum(north, 0.0)
        + jnp.minimum(south, 0.0)
    )
    return jnp.stack(
        [
            here,
            -jnp.minimum(wind_east, 0.0),
            jnp.maximum(west, 0.0),
            -jnp.minimum(north, 0.0),
            jnp.maximum(south, 0.0),
        ]
    )


def first_body(offs, weights, c, coef, below, above, a_out, up_out, down_out, own_out):
    for tile in range(LONS // 8):
        rows = slice(8 * tile, 8 * tile + 8)
        q = c[rows, :]
        acc = coef[0:1, :] * q
        acc += coef[1:2, :] * pltpu.roll(q, ROWS - 1, 1)
        acc += coef[2:3, :] * pltpu.roll(q, LONS - 1, 1)
        acc += coef[3:4, :] * pltpu.roll(q, 1, 1)
        acc += coef[4:5, :] * pltpu.roll(q, ROWS - (LONS - 1), 1)
        acc += coef[5:6, :] * pltpu.roll(q, ROWS - LONS, 1)
        acc += coef[6:7, :] * pltpu.roll(q, LONS, 1)
        a_out[rows, :] = acc
        a_out[rows, :EDGE] += coef[7:8, :EDGE] * pltpu.roll(below[rows, :], LONS, 1)
        a_out[rows, EDGE_START:] += coef[7:8, EDGE_START:] * pltpu.roll(above[rows, :], EDGE_LOW, 1)
    for k in range(PER_SLAB):
        up_out[k : k + 1, :] = a_out[pl.ds(offs[2 * PER_SLAB + k], 1), :]
        down_out[k : k + 1, :] = a_out[pl.ds(offs[k], 1), :]
        o = offs[PER_SLAB + k]
        east = jnp.where(o == LONS - 1, 0, o + 1)
        west = jnp.where(o == 0, LONS - 1, o - 1)
        own_out[k : k + 1, :] = (
            weights[0, k] * a_out[pl.ds(o, 1), :]
            + weights[1, k] * a_out[pl.ds(east, 1), :]
            + weights[2, k] * a_out[pl.ds(west, 1), :]
        )
    for ref in (up_out, down_out, own_out):
        ref[PER_SLAB:8, :] = jnp.zeros((8 - PER_SLAB, ROWS), F32)


def observed_body(weights, own, north, south, index, rows_out, block_out):
    for k in range(PER_SLAB):
        rows_out[k : k + 1, :] = (
            own[k : k + 1, :]
            + weights[3, k] * north[k : k + 1, :]
            + weights[4, k] * south[k : k + 1, :]
        )
    width = ROWS // 5
    total = jnp.zeros((8, BLOCK), F32)
    for part in range(5):
        lanes = lax.broadcasted_iota(jnp.int32, (width, BLOCK), 0) + part * width
        picked = (lanes == index[...]).astype(F32)
        rows = jnp.concatenate(
            [rows_out[:, part * width : (part + 1) * width], jnp.zeros((2, width), F32)], axis=0
        )
        total += mm(rows, picked)
    block_out[...] = total[:PER_SLAB, :PER_BAND]


def second_body(coef, a, north, south, index, f_out, picked_out, total):
    step = pl.program_id(0)
    q = a[...]
    acc = coef[:, 0:1] * q
    acc += coef[:, 1:2] * pltpu.roll(q, LONS - 1, 0)
    acc += coef[:, 2:3] * pltpu.roll(q, 1, 0)
    acc += coef[:, 3:4] * north[...]
    acc += coef[:, 4:5] * south[...]
    f_out[...] = acc
    width = acc.shape[1]
    lanes = lax.broadcasted_iota(jnp.int32, (width, BLOCK), 0) + step * width
    part = mm(acc, (lanes == index[...]).astype(F32))

    @pl.when(step == 0)
    def _():
        total[...] = part

    @pl.when(step > 0)
    def _():
        total[...] += part

    @pl.when(step == pl.num_programs(0) - 1)
    def _():
        picked_out[...] = total[:, :PER_BAND]


def inverse_2(a, b, d):
    scale = 1.0 / (a * d - b * b)
    return d * scale, -b * scale, a * scale


def inverse_block(m):
    n = BLOCK
    lane = lax.broadcasted_iota(jnp.int32, (8, n), 1)
    sub = lax.broadcasted_iota(jnp.int32, (8, n), 0)
    tiles = [m[8 * t : 8 * t + 8, :] for t in range(n // 8)]
    for j in range(0, n, 4):
        home, base = j // 8, j % 8
        columns = [
            [
                jnp.take_along_axis(tile, jnp.full((8, n), j + k, jnp.int32), axis=1)
                for k in range(4)
            ]
            for tile in tiles
        ]
        p = [
            [
                jnp.broadcast_to(columns[home][k][base + i : base + i + 1, :], (8, n))
                for k in range(4)
            ]
            for i in range(4)
        ]
        a00, a01, a11 = inverse_2(p[0][0], p[0][1], p[1][1])
        y00 = a00 * p[0][2] + a01 * p[1][2]
        y01 = a00 * p[0][3] + a01 * p[1][3]
        y10 = a01 * p[0][2] + a11 * p[1][2]
        y11 = a01 * p[0][3] + a11 * p[1][3]
        s00 = p[2][2] - (p[0][2] * y00 + p[1][2] * y10)
        s01 = p[2][3] - (p[0][2] * y01 + p[1][2] * y11)
        s11 = p[3][3] - (p[0][3] * y01 + p[1][3] * y11)
        d00, d01, d11 = inverse_2(s00, s01, s11)
        z00 = y00 * d00 + y01 * d01
        z01 = y00 * d01 + y01 * d11
        z10 = y10 * d00 + y11 * d01
        z11 = y10 * d01 + y11 * d11
        b00 = a00 + z00 * y00 + z01 * y01
        b01 = a01 + z00 * y10 + z01 * y11
        b11 = a11 + z10 * y10 + z11 * y11
        inv = [
            [b00, b01, -z00, -z01],
            [b01, b11, -z10, -z11],
            [-z00, -z10, d00, d01],
            [-z01, -z11, d01, d11],
        ]
        rows = [
            jnp.where(
                (lane >= j) & (lane < j + 4),
                jnp.where(lane == j + i, 1.0, 0.0),
                jnp.broadcast_to(tiles[home][base + i : base + i + 1, :], (8, n)),
            )
            for i in range(4)
        ]
        t = [
            (inv[i][0] * rows[0] + inv[i][1] * rows[1]) + (inv[i][2] * rows[2] + inv[i][3] * rows[3])
            for i in range(4)
        ]
        swept = []
        for number, tile in enumerate(tiles):
            col = columns[number]
            kept = jnp.where((lane >= j) & (lane < j + 4), 0.0, tile)
            new = kept - ((col[0] * t[0] + col[1] * t[1]) + (col[2] * t[2] + col[3] * t[3]))
            if number == home:
                for i in range(4):
                    new = jnp.where(sub == base + i, t[i], new)
            swept.append(new)
        tiles = swept
    return jnp.concatenate(tiles, axis=0)


def inverse_body(blocks, noise, out):
    for b in range(BANDS):
        out[:, b * PER_BAND : (b + 1) * PER_BAND] = blocks[b]
    r = lax.broadcasted_iota(jnp.int32, (OBS, OBS), 0)
    c = lax.broadcasted_iota(jnp.int32, (OBS, OBS), 1)
    out[...] += jnp.where(r == c, noise[...], 0.0)

    def sweep(step, carry):
        at = pl.multiple_of(step * BLOCK, BLOCK)
        inv = inverse_block(out[pl.ds(at, BLOCK), pl.ds(at, BLOCK)])
        column = out[:, pl.ds(at, BLOCK)]
        row_id = lax.broadcasted_iota(jnp.int32, (OBS, BLOCK), 0)
        column = jnp.where((row_id >= at) & (row_id < at + BLOCK), 0.0, column)
        out[:, pl.ds(at, BLOCK)] = jnp.zeros((OBS, BLOCK), F32)
        top = mm(inv, out[pl.ds(at, BLOCK), :])
        out[pl.ds(at, BLOCK), :] = top
        out[pl.ds(at, BLOCK), pl.ds(at, BLOCK)] = inv
        top = out[pl.ds(at, BLOCK), :]
        out[...] -= mm(column, top)
        return carry

    lax.fori_loop(0, OBS // BLOCK, sweep, 0)


def update_body(core, picked, inverse, order, f, mine, other, out, gain, wide):
    @pl.when(pl.program_id(0) == 0)
    def _():
        for b in range(BANDS):
            wide[:, b * PER_BAND : (b + 1) * PER_BAND] = picked[b]
        gain[...] = mm(mm(wide[...], inverse[...]), order[...])

    mine_first = core[0] == 0
    a, b = mine[...], other[...]
    rows = jnp.concatenate([jnp.where(mine_first, a, b), jnp.where(mine_first, b, a)], axis=0)
    out[...] = f[...] - mm(gain[...], rows)


def vmem():
    return pl.BlockSpec(memory_space=pltpu.VMEM)


def smem():
    return pl.BlockSpec(memory_space=pltpu.SMEM)


def shape(*dims):
    return jax.ShapeDtypeStruct(dims, F32)


def split_col(c):
    return c // 16, (c // 2) % 8, c % 2


def col_groups(key):
    groups = {}
    for c in range(SLABS):
        groups.setdefault(key(*split_col(c)), []).append(c)
    return [groups[k] for k in sorted(groups)]


def to_all(shard, axis, count, groups=None):
    return lax.all_to_all(
        jnp.broadcast_to(shard[None], (count, *shard.shape)),
        axis,
        0,
        0,
        tiled=True,
        axis_index_groups=groups,
    )


def local(covariance, wind_east, wind_north, obs_owner, obs_offset, obs_variance):
    band = lax.axis_index("band")
    col = lax.axis_index("col")
    core = col % 2
    same = obs_owner[:, :, None] == obs_owner[:, None, :]
    earlier = jnp.arange(128)[None, :] < jnp.arange(128)[:, None]
    place = jnp.sum((same & earlier[None]).astype(jnp.int32), axis=2)
    slot = obs_owner * 2 + place
    hit = slot[:, None, :] == jnp.arange(2 * SLABS)[None, :, None]
    offsets = jnp.sum(jnp.where(hit, obs_offset[:, None, :], 0), axis=2)
    noise = jnp.sum(jnp.where(hit, obs_variance[:, None, :], 0.0), axis=2)
    by_slab = lambda v: v.reshape(BATCHES, SLABS, 2).transpose(1, 0, 2).reshape(SLABS, PER_SLAB)
    offsets, noise = by_slab(offsets), by_slab(noise)

    table = stencil(wind_east, wind_north)
    lat_coef = lax.dynamic_slice_in_dim(table, band * STRIP, STRIP, 1).reshape(5, ROWS)
    lane = jnp.arange(ROWS)
    lon = lane % LONS
    first_coef = jnp.stack(
        [
            lat_coef[0],
            jnp.where(lon < LONS - 1, lat_coef[1], 0.0),
            jnp.where(lon == LONS - 1, lat_coef[1], 0.0),
            jnp.where(lon > 0, lat_coef[2], 0.0),
            jnp.where(lon == 0, lat_coef[2], 0.0),
            jnp.where(lane < ROWS - LONS, lat_coef[3], 0.0),
            jnp.where(lane >= LONS, lat_coef[4], 0.0),
            jnp.where(lane < LONS, lat_coef[4], jnp.where(lane >= ROWS - LONS, lat_coef[3], 0.0)),
        ]
    )
    slab_coef = lax.dynamic_slice_in_dim(table, col, 1, 1)[:, 0]
    second_coef = jnp.pad(slab_coef, ((0, 3), (0, 0))).T
    near = jnp.concatenate([offsets[-1:], offsets, offsets[:1]], axis=0)
    near = lax.dynamic_slice_in_dim(near, col, 3, 0)
    own_offsets = near[1]
    weights = jnp.take(slab_coef, own_offsets, axis=1)
    band_points = (
        lax.dynamic_slice_in_dim(offsets, band * STRIP, STRIP, 0)
        + jnp.arange(STRIP)[:, None] * LONS
    ).reshape(1, PER_BAND)
    index = jnp.pad(band_points, ((0, 0), (0, BLOCK - PER_BAND)), constant_values=-1)

    up_band = [(i, i + 1) for i in range(BANDS - 1)]
    down_band = [(i + 1, i) for i in range(BANDS - 1)]
    up_col = [(i, i + 1) for i in range(SLABS - 1)]
    down_col = [(i + 1, i) for i in range(SLABS - 1)]
    below = lax.ppermute(covariance[:, EDGE_START:], "band", up_band)
    above = lax.ppermute(covariance[:, :EDGE], "band", down_band)

    advected, for_up, for_down, own = pl.pallas_call(
        first_body,
        out_shape=[shape(LONS, ROWS)] + [shape(8, ROWS)] * 3,
        in_specs=[smem(), smem()] + [vmem()] * 4,
        out_specs=[vmem()] * 4,
        name="first",
    )(near.reshape(-1), weights, covariance, first_coef, below, above)

    south_rows = lax.ppermute(for_up, "col", up_col)
    north_rows = lax.ppermute(for_down, "col", down_col)
    south_slab = lax.ppermute(advected, "col", up_col)
    north_slab = lax.ppermute(advected, "col", down_col)

    observed, block = pl.pallas_call(
        observed_body,
        out_shape=[shape(PER_SLAB, ROWS), shape(PER_SLAB, PER_BAND)],
        in_specs=[smem()] + [vmem()] * 4,
        out_specs=[vmem()] * 2,
        name="observed",
    )(weights, own, north_rows, south_rows, index)

    blocks = to_all(block, ("band", "col"), BANDS * SLABS).reshape(BANDS, OBS, PER_BAND)
    across_x = to_all(observed, "col", 4, col_groups(lambda x, z, k: (z, k)))
    across_x = across_x.reshape(4 * PER_SLAB, ROWS)
    mine = to_all(across_x, "col", 8, col_groups(lambda x, z, k: (x, k))).reshape(HALF, ROWS)
    other = lax.ppermute(mine, "col", [(c, c ^ 1) for c in range(SLABS)])

    width = ROWS // 5
    forecast, picked = pl.pallas_call(
        second_body,
        out_shape=[shape(LONS, ROWS), shape(LONS, PER_BAND)],
        grid=(5,),
        in_specs=[pl.BlockSpec((LONS, 8), lambda i: (0, 0))]
        + [pl.BlockSpec((LONS, width), lambda i: (0, i))] * 3
        + [pl.BlockSpec((1, BLOCK), lambda i: (0, 0))],
        out_specs=[
            pl.BlockSpec((LONS, width), lambda i: (0, i)),
            pl.BlockSpec((LONS, PER_BAND), lambda i: (0, 0)),
        ],
        scratch_shapes=[pltpu.VMEM((LONS, BLOCK), F32)],
        name="second",
    )(second_coef, advected, north_slab, south_slab, index)
    picked_all = to_all(picked, "band", BANDS)

    inverse = pl.pallas_call(
        inverse_body,
        out_shape=shape(OBS, OBS),
        in_specs=[vmem()] * 2,
        out_specs=vmem(),
        name="inverse",
    )(blocks, noise.reshape(1, OBS))

    n = jnp.arange(OBS)
    arrival = (n // 24 % 8) * 12 + (n // HALF) * 6 + (n // 6 % 4) * PER_BAND + n % 6
    order = (n[:, None] == arrival[None, :]).astype(F32)
    return pl.pallas_call(
        update_body,
        out_shape=shape(LONS, ROWS),
        grid=(5,),
        in_specs=[
            smem(),
            pl.BlockSpec((BANDS, LONS, PER_BAND), lambda i: (0, 0, 0)),
            pl.BlockSpec((OBS, OBS), lambda i: (0, 0)),
            pl.BlockSpec((OBS, OBS), lambda i: (0, 0)),
            pl.BlockSpec((LONS, width), lambda i: (0, i)),
            pl.BlockSpec((HALF, width), lambda i: (0, i)),
            pl.BlockSpec((HALF, width), lambda i: (0, i)),
        ],
        out_specs=pl.BlockSpec((LONS, width), lambda i: (0, i)),
        scratch_shapes=[pltpu.VMEM((LONS, OBS), F32), pltpu.VMEM((LONS, OBS), F32)],
        name="update",
    )(core.reshape(1), picked_all, inverse, order, forecast, mine, other)


def solution(mesh):
    return jax.shard_map(
        local,
        mesh=mesh,
        in_specs=(P("col", "band"), P(), P(), P(), P(), P()),
        out_specs=P("col", "band"),
        check_vma=False,
    )
```

```python
from functools import partial

import jax
import jax.numpy as jnp
from jax import lax
from jax.experimental import pallas as pl
from jax.experimental.pallas import tpu as pltpu
from jax.sharding import PartitionSpec as P


LATS = 64
LONS = 160
BANDS = 4
SLABS = 64
STRIP = LATS // BANDS
ROWS = STRIP * LONS
BATCHES = 3
PER_SLAB = 6
OBS = SLABS * PER_SLAB
PER_BAND = OBS // BANDS
EDGE = 256
EDGE_START = ROWS - EDGE
EDGE_LOW = EDGE - LONS
HALF = OBS // 2
SIDE = ROWS // 2
CHUNK = SIDE // 2
BLOCK = 128
HIGHEST = lax.Precision.HIGHEST
F32 = jnp.float32


def mm(a, b):
    return lax.dot_general(
        a, b, (((1,), (0,)), ((), ())), precision=HIGHEST, preferred_element_type=F32
    )


def stencil(east, west, north, south):
    here = (
        1.0
        - jnp.maximum(east, 0.0)
        + jnp.minimum(west, 0.0)
        - jnp.maximum(north, 0.0)
        + jnp.minimum(south, 0.0)
    )
    return [
        here,
        -jnp.minimum(east, 0.0),
        jnp.maximum(west, 0.0),
        -jnp.minimum(north, 0.0),
        jnp.maximum(south, 0.0),
    ]


def westward(wind):
    return jnp.concatenate([wind[:, LONS - 1 :], wind[:, : LONS - 1]], axis=1)


def prepare_body(
    place, owner, offset, variance, wind_east, wind_north,
    near_out, index_out, noise_out, first_out, second_out, weights_out,
):
    band, col = place[0], place[1]
    sub = lax.broadcasted_iota(jnp.int32, (BLOCK, BLOCK), 0)
    lane = lax.broadcasted_iota(jnp.int32, (BLOCK, BLOCK), 1)
    target = lax.broadcasted_iota(jnp.int32, (BLOCK, OBS), 1)
    natural = jnp.zeros((1, OBS), jnp.int32)
    offsets = jnp.zeros((1, OBS), jnp.int32)
    noise = jnp.zeros((1, OBS), F32)

    def tall(row):
        return jnp.transpose(jnp.broadcast_to(row, (BLOCK, BLOCK)))

    def wide(v):
        return jnp.concatenate([v] * BATCHES, axis=1)

    for t in range(BATCHES):
        row = owner[t : t + 1, :]
        flat = jnp.broadcast_to(row, (BLOCK, BLOCK))
        same = (flat == jnp.transpose(flat)) & (sub < lane)
        rank = jnp.sum(same.astype(jnp.int32), axis=0, keepdims=True)
        within = 2 * t + rank
        plain = wide(tall(row * PER_SLAB + within)) == target
        lanes = (row // 16) * PER_BAND + (row & 1) * 48 + (row // 2 % 8) * PER_SLAB + within
        hit = wide(tall(lanes)) == target
        away = wide(tall(offset[t : t + 1, :]))
        natural += jnp.sum(jnp.where(plain, away, 0), axis=0, keepdims=True)
        offsets += jnp.sum(jnp.where(hit, away, 0), axis=0, keepdims=True)
        noise += jnp.sum(
            jnp.where(hit, wide(tall(variance[t : t + 1, :])), 0.0), axis=0, keepdims=True
        )
    noise_out[...] = noise
    spread = jnp.broadcast_to(natural, (8, OBS))
    shift = (SLABS + 1 - col) * PER_SLAB
    near = pltpu.roll(spread, lax.rem(shift, OBS), 1)[:, :BLOCK]
    near_out[...] = near
    n = lax.broadcasted_iota(jnp.int32, (8, OBS), 1)
    slab = (n // PER_SLAB % 8) * 2 + n // 48 % 2
    spread = jnp.broadcast_to(offsets, (8, OBS)) + slab * LONS
    points = pltpu.roll(spread, lax.rem(OBS - band * PER_BAND, OBS), 1)[0:1, :BLOCK]
    index_out[...] = jnp.where(lane[0:1, :] < PER_BAND, points, -1)

    start = pl.multiple_of(band * STRIP, STRIP)
    lat = lax.broadcasted_iota(jnp.int32, (STRIP, LONS), 0)
    lon = lax.broadcasted_iota(jnp.int32, (STRIP, LONS), 1)
    east = wind_east[pl.ds(start, STRIP), :]
    north = wind_north[pl.ds(start, STRIP), :]
    before = wind_north[pl.ds(jnp.maximum(band * STRIP - 1, 0), 1), :]
    south = jnp.concatenate([before, north[: STRIP - 1]], axis=0)
    south = jnp.where(lat + start == 0, 0.0, south)
    north = jnp.where(lat + start == LATS - 1, 0.0, north)
    here, to_east, to_west, to_north, to_south = stencil(east, westward(east), north, south)
    kinds = [
        here,
        jnp.where(lon < LONS - 1, to_east, 0.0),
        jnp.where(lon == LONS - 1, to_east, 0.0),
        jnp.where(lon > 0, to_west, 0.0),
        jnp.where(lon == 0, to_west, 0.0),
        jnp.where(lat < STRIP - 1, to_north, 0.0),
        jnp.where(lat > 0, to_south, 0.0),
        jnp.where(lat == 0, to_south, jnp.where(lat == STRIP - 1, to_north, 0.0)),
    ]
    for r in range(STRIP):
        first_out[:, r * LONS : (r + 1) * LONS] = jnp.concatenate(
            [kind[r : r + 1, :] for kind in kinds], axis=0
        )

    east = wind_east[pl.ds(col, 1), :]
    north = wind_north[pl.ds(col, 1), :]
    south = wind_north[pl.ds(jnp.maximum(col - 1, 0), 1), :]
    north = jnp.where(col == LATS - 1, 0.0, north)
    south = jnp.where(col == 0, 0.0, south)
    slab_coef = jnp.concatenate(
        stencil(east, westward(east), north, south) + [jnp.zeros((3, LONS), F32)], axis=0
    )
    second_out[...] = slab_coef
    own = pltpu.roll(near, BLOCK - PER_SLAB, 1)[0:1, :]
    picked = (lax.broadcasted_iota(jnp.int32, (LONS, BLOCK), 0) == own).astype(F32)
    weights = mm(slab_coef, picked)
    weights = jnp.concatenate([weights, jnp.zeros((BLOCK - 8, BLOCK), F32)], axis=0)
    weights_out[...] = jnp.transpose(weights)[:8, :]


def tiles_to_row(v):
    return jnp.concatenate([v[8 * t : 8 * t + 8, :] for t in range(LONS // 8)], axis=1)


def row_to_tiles(v):
    return jnp.concatenate([v[:, BLOCK * t : BLOCK * (t + 1)] for t in range(LONS // 8)], axis=0)


def first_body(near, weights, c, coef, below, above, index, a_out, up_out, down_out, own_out, pair):
    for tile in range(LONS // 8):
        rows = slice(8 * tile, 8 * tile + 8)
        q = c[rows, :]
        acc = coef[0:1, :] * q
        acc += coef[1:2, :] * pltpu.roll(q, ROWS - 1, 1)
        acc += coef[2:3, :] * pltpu.roll(q, LONS - 1, 1)
        acc += coef[3:4, :] * pltpu.roll(q, 1, 1)
        acc += coef[4:5, :] * pltpu.roll(q, ROWS - (LONS - 1), 1)
        acc += coef[5:6, :] * pltpu.roll(q, ROWS - LONS, 1)
        acc += coef[6:7, :] * pltpu.roll(q, LONS, 1)
        a_out[rows, :] = acc
        a_out[rows, :EDGE] += coef[7:8, :EDGE] * pltpu.roll(below[rows, :], LONS, 1)
        a_out[rows, EDGE_START:] += coef[7:8, EDGE_START:] * pltpu.roll(above[rows, :], EDGE_LOW, 1)
    up_out[:8, :] = jnp.zeros((8, ROWS), F32)
    down_out[:8, :] = jnp.zeros((8, ROWS), F32)
    own_out[:8, :] = jnp.zeros((8, ROWS), F32)
    pair[...] = jnp.zeros(pair.shape, F32)
    for k in range(PER_SLAB):
        up_out[k : k + 1, :] = a_out[pl.ds(near[0, 2 * PER_SLAB + k], 1), :]
        down_out[k : k + 1, :] = a_out[pl.ds(near[0, k], 1), :]
        o = near[0, PER_SLAB + k]
        own_out[k : k + 1, :] = a_out[pl.ds(o, 1), :]
        pair[k : k + 1, :] = a_out[pl.ds(jnp.where(o == LONS - 1, 0, o + 1), 1), :]
        pair[k + 8 : k + 9, :] = a_out[pl.ds(jnp.where(o == 0, LONS - 1, o - 1), 1), :]
    own_out[:8, :] = (
        weights[:, 0:1] * own_out[:8, :]
        + weights[:, 1:2] * pair[:8, :]
        + weights[:, 2:3] * pair[8:, :]
    )
    width = ROWS // 5
    total = jnp.zeros((LONS, BLOCK), F32)
    for part in range(5):
        lanes = lax.broadcasted_iota(jnp.int32, (width, BLOCK), 0) + part * width
        picked = (lanes == index[...]).astype(F32)
        total += mm(a_out[:, part * width : (part + 1) * width], picked)
    packed = tiles_to_row(total)
    for ref in (up_out, down_out, own_out):
        ref[8:, :] = packed


def observed_body(weights, coef, own, north, south, index, rows_out, picked_out):
    rows = own[:8, :] + weights[:, 3:4] * north[:8, :] + weights[:, 4:5] * south[:8, :]
    rows_out[:, :ROWS] = rows[:PER_SLAB, :]
    width = ROWS // 5
    total = jnp.zeros((8, BLOCK), F32)
    for part in range(5):
        lanes = lax.broadcasted_iota(jnp.int32, (width, BLOCK), 0) + part * width
        picked = (lanes == index[...]).astype(F32)
        total += mm(rows[:, part * width : (part + 1) * width], picked)
    rows_out[:, ROWS:] = total[:PER_SLAB, :]
    q = row_to_tiles(own[8:, :])
    picked = second_step(coef, q, row_to_tiles(north[8:, :]), row_to_tiles(south[8:, :]))
    picked_out[...] = picked[:, :PER_BAND]


def second_step(coef, q, north, south):
    return (
        coef[:, 0:1] * q
        + coef[:, 1:2] * pltpu.roll(q, LONS - 1, 0)
        + coef[:, 2:3] * pltpu.roll(q, 1, 0)
        + coef[:, 3:4] * north
        + coef[:, 4:5] * south
    )


def inverse_2(a, b, d):
    scale = 1.0 / (a * d - b * b)
    return d * scale, -b * scale, a * scale


def inverse_block(m):
    n = BLOCK
    lane = lax.broadcasted_iota(jnp.int32, (8, n), 1)
    sub = lax.broadcasted_iota(jnp.int32, (8, n), 0)
    tiles = [m[8 * t : 8 * t + 8, :] for t in range(n // 8)]
    for j in range(0, n, 4):
        home, base = j // 8, j % 8
        columns = [
            [
                jnp.take_along_axis(tile, jnp.full((8, n), j + k, jnp.int32), axis=1)
                for k in range(4)
            ]
            for tile in tiles
        ]
        p = [
            [
                jnp.broadcast_to(columns[home][k][base + i : base + i + 1, :], (8, n))
                for k in range(4)
            ]
            for i in range(4)
        ]
        a00, a01, a11 = inverse_2(p[0][0], p[0][1], p[1][1])
        y00 = a00 * p[0][2] + a01 * p[1][2]
        y01 = a00 * p[0][3] + a01 * p[1][3]
        y10 = a01 * p[0][2] + a11 * p[1][2]
        y11 = a01 * p[0][3] + a11 * p[1][3]
        s00 = p[2][2] - (p[0][2] * y00 + p[1][2] * y10)
        s01 = p[2][3] - (p[0][2] * y01 + p[1][2] * y11)
        s11 = p[3][3] - (p[0][3] * y01 + p[1][3] * y11)
        d00, d01, d11 = inverse_2(s00, s01, s11)
        z00 = y00 * d00 + y01 * d01
        z01 = y00 * d01 + y01 * d11
        z10 = y10 * d00 + y11 * d01
        z11 = y10 * d01 + y11 * d11
        b00 = a00 + z00 * y00 + z01 * y01
        b01 = a01 + z00 * y10 + z01 * y11
        b11 = a11 + z10 * y10 + z11 * y11
        inv = [
            [b00, b01, -z00, -z01],
            [b01, b11, -z10, -z11],
            [-z00, -z10, d00, d01],
            [-z01, -z11, d01, d11],
        ]
        rows = [
            jnp.where(
                (lane >= j) & (lane < j + 4),
                jnp.where(lane == j + i, 1.0, 0.0),
                jnp.broadcast_to(tiles[home][base + i : base + i + 1, :], (8, n)),
            )
            for i in range(4)
        ]
        t = [
            (inv[i][0] * rows[0] + inv[i][1] * rows[1]) + (inv[i][2] * rows[2] + inv[i][3] * rows[3])
            for i in range(4)
        ]
        swept = []
        for number, tile in enumerate(tiles):
            col = columns[number]
            kept = jnp.where((lane >= j) & (lane < j + 4), 0.0, tile)
            new = kept - ((col[0] * t[0] + col[1] * t[1]) + (col[2] * t[2] + col[3] * t[3]))
            if number == home:
                for i in range(4):
                    new = jnp.where(sub == base + i, t[i], new)
            swept.append(new)
        tiles = swept
    return jnp.concatenate(tiles, axis=0)


def sweep(out, at):
    inv = inverse_block(out[at : at + BLOCK, at : at + BLOCK])
    row_id = lax.broadcasted_iota(jnp.int32, (OBS, BLOCK), 0)
    column = out[:, at : at + BLOCK]
    column = jnp.where((row_id >= at) & (row_id < at + BLOCK), 0.0, column)
    out[:, at : at + BLOCK] = jnp.zeros((OBS, BLOCK), F32)
    top = mm(inv, out[at : at + BLOCK, :])
    lane = lax.broadcasted_iota(jnp.int32, (BLOCK, OBS), 1)
    inv_wide = jnp.concatenate([inv] * (OBS // BLOCK), axis=1)
    top = jnp.where((lane >= at) & (lane < at + BLOCK), inv_wide, top)
    out[at : at + BLOCK, :] = top
    out[...] -= mm(column, top)


def inverse_first_body(blocks, noise, out):
    for b in range(BANDS):
        for x in range(BANDS):
            for core in range(2):
                at = (x * 2 + core) * 48
                out[at : at + 48, b * PER_BAND : (b + 1) * PER_BAND] = blocks[
                    (b * BANDS + x) * 2 + core
                ]
    r = lax.broadcasted_iota(jnp.int32, (OBS, OBS), 0)
    c = lax.broadcasted_iota(jnp.int32, (OBS, OBS), 1)
    out[...] += jnp.where(r == c, noise[...], 0.0)
    sweep(out, 0)


def inverse_body(at, before, out):
    out[...] = before[...]
    sweep(out, at)


def order_body(place, out):
    col = place[1]
    r = lax.broadcasted_iota(jnp.int32, (OBS, OBS), 0)
    n = lax.broadcasted_iota(jnp.int32, (1, OBS), 1)
    which = (n // HALF + col) & 1
    step = n // 48 % 4
    away = jnp.where(step == 2, 3, jnp.where(step == 3, 2, step))
    arrival = (((col // 16 + away) & 3) * 2 + which) * 48 + n % 48
    out[...] = (r == arrival).astype(F32)


def update_body(picked, inverse, order, coef, a, north, south, *refs):
    pieces, (out, gain, wide) = refs[:8], refs[8:]

    @pl.when(pl.program_id(0) == 0)
    def _():
        for b in range(BANDS):
            wide[:, b * PER_BAND : (b + 1) * PER_BAND] = picked[b]
        gain[...] = mm(mm(wide[...], inverse[...]), order[...])

    rows = jnp.concatenate([piece[...] for piece in pieces], axis=0)
    out[...] = second_step(coef, a[...], north[...], south[...]) - mm(gain[...], rows)


def vmem():
    return pl.BlockSpec(memory_space=pltpu.VMEM)


def smem():
    return pl.BlockSpec(memory_space=pltpu.SMEM)


def shape(*dims):
    return jax.ShapeDtypeStruct(dims, F32)


def split_col(c):
    return c // 16, (c // 2) % 8, c % 2


def col_groups(key):
    groups = {}
    for c in range(SLABS):
        groups.setdefault(key(*split_col(c)), []).append(c)
    return [groups[k] for k in sorted(groups)]


def to_all(shard, axis, count, groups=None):
    return lax.all_to_all(
        jnp.broadcast_to(shard[None], (count, *shard.shape)),
        axis,
        0,
        0,
        tiled=True,
        axis_index_groups=groups,
    )


def local(covariance, wind_east, wind_north, obs_owner, obs_offset, obs_variance):
    band = lax.axis_index("band")
    col = lax.axis_index("col")
    place = jnp.stack([band, col])

    up_band = [(i, i + 1) for i in range(BANDS - 1)]
    down_band = [(i + 1, i) for i in range(BANDS - 1)]
    up_col = [(i, i + 1) for i in range(SLABS - 1)]
    down_col = [(i + 1, i) for i in range(SLABS - 1)]
    below = lax.ppermute(covariance[:, EDGE_START:], "band", up_band)
    above = lax.ppermute(covariance[:, :EDGE], "band", down_band)

    near, index, noise, first_coef, slab_coef, weights = pl.pallas_call(
        prepare_body,
        out_shape=[
            jax.ShapeDtypeStruct((8, BLOCK), jnp.int32),
            jax.ShapeDtypeStruct((1, BLOCK), jnp.int32),
            shape(1, OBS),
            shape(8, ROWS),
            shape(8, LONS),
            shape(8, BLOCK),
        ],
        in_specs=[smem()] + [vmem()] * 5,
        out_specs=[vmem()] * 6,
        name="prepare",
    )(place, obs_owner, obs_offset, obs_variance, wind_east, wind_north)

    advected, for_up, for_down, own = pl.pallas_call(
        first_body,
        out_shape=[shape(LONS, ROWS)] + [shape(16, ROWS)] * 3,
        in_specs=[smem()] + [vmem()] * 6,
        out_specs=[vmem()] * 4,
        scratch_shapes=[pltpu.VMEM((16, ROWS), F32)],
        name="first",
    )(near, weights, covariance, first_coef, below, above, index)

    south_rows = lax.ppermute(for_up, "col", up_col)
    north_rows = lax.ppermute(for_down, "col", down_col)
    south_slab = lax.ppermute(advected, "col", up_col)
    north_slab = lax.ppermute(advected, "col", down_col)

    second_coef = slab_coef.T
    rows, picked = pl.pallas_call(
        observed_body,
        out_shape=[shape(PER_SLAB, ROWS + BLOCK), shape(LONS, PER_BAND)],
        in_specs=[vmem()] * 6,
        out_specs=[vmem()] * 2,
        name="observed",
    )(weights, second_coef, own, north_rows, south_rows, index)

    rows = to_all(rows, "col", 8, col_groups(lambda x, z, k: (x, k)))
    blocks = rows[:, :, ROWS : ROWS + PER_BAND].reshape(48, PER_BAND)
    rows = rows[:, :, :ROWS].reshape(48, ROWS)
    blocks = to_all(
        blocks,
        ("band", "col"),
        32,
        [
            [b * SLABS + x * 16 + z * 2 + k for b in range(BANDS) for x in range(4) for k in range(2)]
            for z in range(8)
        ],
    )
    pieces = [rows] + [
        lax.ppermute(rows, "col", [(c, (c - 16 * d) % SLABS) for c in range(SLABS)])
        for d in (1, 3, 2)
    ]
    partner = [(c, c ^ 1) for c in range(SLABS)]
    pieces += [lax.ppermute(piece, "col", partner) for piece in pieces]
    picked_all = to_all(picked, "band", BANDS)

    inverse = pl.pallas_call(
        inverse_first_body,
        out_shape=shape(OBS, OBS),
        in_specs=[vmem()] * 2,
        out_specs=vmem(),
        name="inverse_0",
    )(blocks, noise)
    for step in (1, 2):
        inverse = pl.pallas_call(
            partial(inverse_body, step * BLOCK),
            out_shape=shape(OBS, OBS),
            in_specs=[vmem()],
            out_specs=vmem(),
        )(inverse)

    order = pl.pallas_call(
        order_body,
        out_shape=shape(OBS, OBS),
        in_specs=[smem()],
        out_specs=vmem(),
        name="order",
    )(place)
    chunk = lambda height: pl.BlockSpec((height, CHUNK), lambda i: (0, i))
    return pl.pallas_call(
        update_body,
        out_shape=shape(LONS, ROWS),
        grid=(4,),
        in_specs=[
            pl.BlockSpec((BANDS, LONS, PER_BAND), lambda i: (0, 0, 0)),
            pl.BlockSpec((OBS, OBS), lambda i: (0, 0)),
            pl.BlockSpec((OBS, OBS), lambda i: (0, 0)),
            pl.BlockSpec((LONS, 8), lambda i: (0, 0)),
        ]
        + [chunk(LONS)] * 3
        + [chunk(48)] * 8,
        out_specs=chunk(LONS),
        scratch_shapes=[pltpu.VMEM((LONS, OBS), F32), pltpu.VMEM((LONS, OBS), F32)],
        name="update",
    )(picked_all, inverse, order, second_coef, advected, north_slab, south_slab, *pieces)


def solution(mesh):
    return jax.shard_map(
        local,
        mesh=mesh,
        in_specs=(P("col", "band"), P(), P(), P(), P(), P()),
        out_specs=P("col", "band"),
        check_vma=False,
    )
```

```python
from functools import partial

import jax
import jax.numpy as jnp
from jax import lax
from jax.experimental import pallas as pl
from jax.experimental.pallas import tpu as pltpu
from jax.sharding import PartitionSpec as P


LATS = 64
LONS = 160
BANDS = 4
SLABS = 64
STRIP = LATS // BANDS
ROWS = STRIP * LONS
BATCHES = 3
PER_SLAB = 6
OBS = SLABS * PER_SLAB
PER_BAND = OBS // BANDS
EDGE = 256
EDGE_START = ROWS - EDGE
EDGE_LOW = EDGE - LONS
HALF = OBS // 2
SIDE = ROWS // 2
CHUNK = SIDE // 2
BLOCK = 128
HIGHEST = lax.Precision.HIGHEST
F32 = jnp.float32


def mm(a, b):
    return lax.dot_general(
        a, b, (((1,), (0,)), ((), ())), precision=HIGHEST, preferred_element_type=F32
    )


def stencil(east, west, north, south):
    here = (
        1.0
        - jnp.maximum(east, 0.0)
        + jnp.minimum(west, 0.0)
        - jnp.maximum(north, 0.0)
        + jnp.minimum(south, 0.0)
    )
    return [
        here,
        -jnp.minimum(east, 0.0),
        jnp.maximum(west, 0.0),
        -jnp.minimum(north, 0.0),
        jnp.maximum(south, 0.0),
    ]


def westward(wind):
    return jnp.concatenate([wind[:, LONS - 1 :], wind[:, : LONS - 1]], axis=1)


def prepare_body(
    place, owner, offset, variance, wind_east, wind_north,
    near_out, index_out, noise_out, first_out, second_out, weights_out,
):
    band, col = place[0], place[1]
    sub = lax.broadcasted_iota(jnp.int32, (BLOCK, BLOCK), 0)
    lane = lax.broadcasted_iota(jnp.int32, (BLOCK, BLOCK), 1)
    target = lax.broadcasted_iota(jnp.int32, (BLOCK, OBS), 1)
    offsets = jnp.zeros((1, OBS), jnp.int32)
    noise = jnp.zeros((1, OBS), F32)

    def tall(row):
        return jnp.transpose(jnp.broadcast_to(row, (BLOCK, BLOCK)))

    def wide(v):
        return jnp.concatenate([v] * BATCHES, axis=1)

    for t in range(BATCHES):
        row = owner[t : t + 1, :]
        flat = jnp.broadcast_to(row, (BLOCK, BLOCK))
        same = (flat == jnp.transpose(flat)) & (sub < lane)
        rank = jnp.sum(same.astype(jnp.int32), axis=0, keepdims=True)
        hit = wide(tall(row * PER_SLAB + 2 * t + rank)) == target
        offsets += jnp.sum(
            jnp.where(hit, wide(tall(offset[t : t + 1, :])), 0), axis=0, keepdims=True
        )
        noise += jnp.sum(
            jnp.where(hit, wide(tall(variance[t : t + 1, :])), 0.0), axis=0, keepdims=True
        )
    noise_out[...] = noise
    spread = jnp.broadcast_to(offsets, (8, OBS))
    shift = (SLABS + 1 - col) * PER_SLAB
    near = pltpu.roll(spread, lax.rem(shift, OBS), 1)[:, :BLOCK]
    near_out[...] = near
    slab = lax.broadcasted_iota(jnp.int32, (8, OBS), 1) // PER_SLAB - band * STRIP
    points = pltpu.roll(spread + slab * LONS, lax.rem(OBS - band * PER_BAND, OBS), 1)[0:1, :BLOCK]
    index_out[...] = jnp.where(lane[0:1, :] < PER_BAND, points, -1)

    start = pl.multiple_of(band * STRIP, STRIP)
    lat = lax.broadcasted_iota(jnp.int32, (STRIP, LONS), 0)
    lon = lax.broadcasted_iota(jnp.int32, (STRIP, LONS), 1)
    east = wind_east[pl.ds(start, STRIP), :]
    north = wind_north[pl.ds(start, STRIP), :]
    before = wind_north[pl.ds(jnp.maximum(band * STRIP - 1, 0), 1), :]
    south = jnp.concatenate([before, north[: STRIP - 1]], axis=0)
    south = jnp.where(lat + start == 0, 0.0, south)
    north = jnp.where(lat + start == LATS - 1, 0.0, north)
    here, to_east, to_west, to_north, to_south = stencil(east, westward(east), north, south)
    kinds = [
        here,
        jnp.where(lon < LONS - 1, to_east, 0.0),
        jnp.where(lon == LONS - 1, to_east, 0.0),
        jnp.where(lon > 0, to_west, 0.0),
        jnp.where(lon == 0, to_west, 0.0),
        jnp.where(lat < STRIP - 1, to_north, 0.0),
        jnp.where(lat > 0, to_south, 0.0),
        jnp.where(lat == 0, to_south, jnp.where(lat == STRIP - 1, to_north, 0.0)),
    ]
    for r in range(STRIP):
        first_out[:, r * LONS : (r + 1) * LONS] = jnp.concatenate(
            [kind[r : r + 1, :] for kind in kinds], axis=0
        )

    east = wind_east[pl.ds(col, 1), :]
    north = wind_north[pl.ds(col, 1), :]
    south = wind_north[pl.ds(jnp.maximum(col - 1, 0), 1), :]
    north = jnp.where(col == LATS - 1, 0.0, north)
    south = jnp.where(col == 0, 0.0, south)
    slab_coef = jnp.concatenate(
        stencil(east, westward(east), north, south) + [jnp.zeros((3, LONS), F32)], axis=0
    )
    second_out[...] = slab_coef
    own = pltpu.roll(near, BLOCK - PER_SLAB, 1)[0:1, :]
    picked = (lax.broadcasted_iota(jnp.int32, (LONS, BLOCK), 0) == own).astype(F32)
    weights = mm(slab_coef, picked)
    weights = jnp.concatenate([weights, jnp.zeros((BLOCK - 8, BLOCK), F32)], axis=0)
    weights_out[...] = jnp.transpose(weights)[:8, :]


def tiles_to_row(v):
    return jnp.concatenate([v[8 * t : 8 * t + 8, :] for t in range(LONS // 8)], axis=1)


def row_to_tiles(v):
    return jnp.concatenate([v[:, BLOCK * t : BLOCK * (t + 1)] for t in range(LONS // 8)], axis=0)


def first_body(near, weights, c, coef, below, above, index, a_out, up_out, down_out, own_out, pair):
    for tile in range(LONS // 8):
        rows = slice(8 * tile, 8 * tile + 8)
        q = c[rows, :]
        acc = coef[0:1, :] * q
        acc += coef[1:2, :] * pltpu.roll(q, ROWS - 1, 1)
        acc += coef[2:3, :] * pltpu.roll(q, LONS - 1, 1)
        acc += coef[3:4, :] * pltpu.roll(q, 1, 1)
        acc += coef[4:5, :] * pltpu.roll(q, ROWS - (LONS - 1), 1)
        acc += coef[5:6, :] * pltpu.roll(q, ROWS - LONS, 1)
        acc += coef[6:7, :] * pltpu.roll(q, LONS, 1)
        a_out[rows, :] = acc
        a_out[rows, :EDGE] += coef[7:8, :EDGE] * pltpu.roll(below[rows, :], LONS, 1)
        a_out[rows, EDGE_START:] += coef[7:8, EDGE_START:] * pltpu.roll(above[rows, :], EDGE_LOW, 1)
    up_out[:8, :] = jnp.zeros((8, ROWS), F32)
    down_out[:8, :] = jnp.zeros((8, ROWS), F32)
    own_out[:8, :] = jnp.zeros((8, ROWS), F32)
    pair[...] = jnp.zeros(pair.shape, F32)
    for k in range(PER_SLAB):
        up_out[k : k + 1, :] = a_out[pl.ds(near[0, 2 * PER_SLAB + k], 1), :]
        down_out[k : k + 1, :] = a_out[pl.ds(near[0, k], 1), :]
        o = near[0, PER_SLAB + k]
        own_out[k : k + 1, :] = a_out[pl.ds(o, 1), :]
        pair[k : k + 1, :] = a_out[pl.ds(jnp.where(o == LONS - 1, 0, o + 1), 1), :]
        pair[k + 8 : k + 9, :] = a_out[pl.ds(jnp.where(o == 0, LONS - 1, o - 1), 1), :]
    own_out[:8, :] = (
        weights[:, 0:1] * own_out[:8, :]
        + weights[:, 1:2] * pair[:8, :]
        + weights[:, 2:3] * pair[8:, :]
    )
    width = ROWS // 5
    total = jnp.zeros((LONS, BLOCK), F32)
    for part in range(5):
        lanes = lax.broadcasted_iota(jnp.int32, (width, BLOCK), 0) + part * width
        picked = (lanes == index[...]).astype(F32)
        total += mm(a_out[:, part * width : (part + 1) * width], picked)
    packed = tiles_to_row(total)
    for ref in (up_out, down_out, own_out):
        ref[8:, :] = packed


def observed_body(weights, coef, own, north, south, index, rows_out, block_out, picked_out):
    rows = own[:8, :] + weights[:, 3:4] * north[:8, :] + weights[:, 4:5] * south[:8, :]
    rows_out[...] = rows[:PER_SLAB, :]
    width = ROWS // 5
    total = jnp.zeros((8, BLOCK), F32)
    for part in range(5):
        lanes = lax.broadcasted_iota(jnp.int32, (width, BLOCK), 0) + part * width
        picked = (lanes == index[...]).astype(F32)
        total += mm(rows[:, part * width : (part + 1) * width], picked)
    block_out[...] = total[:PER_SLAB, :PER_BAND]
    q = row_to_tiles(own[8:, :])
    picked = second_step(coef, q, row_to_tiles(north[8:, :]), row_to_tiles(south[8:, :]))
    picked_out[...] = picked[:, :PER_BAND]


def second_step(coef, q, north, south):
    return (
        coef[:, 0:1] * q
        + coef[:, 1:2] * pltpu.roll(q, LONS - 1, 0)
        + coef[:, 2:3] * pltpu.roll(q, 1, 0)
        + coef[:, 3:4] * north
        + coef[:, 4:5] * south
    )


def inverse_2(a, b, d):
    scale = 1.0 / (a * d - b * b)
    return d * scale, -b * scale, a * scale


def inverse_block(m):
    n = BLOCK
    lane = lax.broadcasted_iota(jnp.int32, (8, n), 1)
    sub = lax.broadcasted_iota(jnp.int32, (8, n), 0)
    tiles = [m[8 * t : 8 * t + 8, :] for t in range(n // 8)]
    for j in range(0, n, 4):
        home, base = j // 8, j % 8
        columns = [
            [
                jnp.take_along_axis(tile, jnp.full((8, n), j + k, jnp.int32), axis=1)
                for k in range(4)
            ]
            for tile in tiles
        ]
        p = [
            [
                jnp.broadcast_to(columns[home][k][base + i : base + i + 1, :], (8, n))
                for k in range(4)
            ]
            for i in range(4)
        ]
        a00, a01, a11 = inverse_2(p[0][0], p[0][1], p[1][1])
        y00 = a00 * p[0][2] + a01 * p[1][2]
        y01 = a00 * p[0][3] + a01 * p[1][3]
        y10 = a01 * p[0][2] + a11 * p[1][2]
        y11 = a01 * p[0][3] + a11 * p[1][3]
        s00 = p[2][2] - (p[0][2] * y00 + p[1][2] * y10)
        s01 = p[2][3] - (p[0][2] * y01 + p[1][2] * y11)
        s11 = p[3][3] - (p[0][3] * y01 + p[1][3] * y11)
        d00, d01, d11 = inverse_2(s00, s01, s11)
        z00 = y00 * d00 + y01 * d01
        z01 = y00 * d01 + y01 * d11
        z10 = y10 * d00 + y11 * d01
        z11 = y10 * d01 + y11 * d11
        b00 = a00 + z00 * y00 + z01 * y01
        b01 = a01 + z00 * y10 + z01 * y11
        b11 = a11 + z10 * y10 + z11 * y11
        inv = [
            [b00, b01, -z00, -z01],
            [b01, b11, -z10, -z11],
            [-z00, -z10, d00, d01],
            [-z01, -z11, d01, d11],
        ]
        rows = [
            jnp.where(
                (lane >= j) & (lane < j + 4),
                jnp.where(lane == j + i, 1.0, 0.0),
                jnp.broadcast_to(tiles[home][base + i : base + i + 1, :], (8, n)),
            )
            for i in range(4)
        ]
        t = [
            (inv[i][0] * rows[0] + inv[i][1] * rows[1]) + (inv[i][2] * rows[2] + inv[i][3] * rows[3])
            for i in range(4)
        ]
        swept = []
        for number, tile in enumerate(tiles):
            col = columns[number]
            kept = jnp.where((lane >= j) & (lane < j + 4), 0.0, tile)
            new = kept - ((col[0] * t[0] + col[1] * t[1]) + (col[2] * t[2] + col[3] * t[3]))
            if number == home:
                for i in range(4):
                    new = jnp.where(sub == base + i, t[i], new)
            swept.append(new)
        tiles = swept
    return jnp.concatenate(tiles, axis=0)


def sweep(out, at):
    inv = inverse_block(out[at : at + BLOCK, at : at + BLOCK])
    row_id = lax.broadcasted_iota(jnp.int32, (OBS, BLOCK), 0)
    column = out[:, at : at + BLOCK]
    column = jnp.where((row_id >= at) & (row_id < at + BLOCK), 0.0, column)
    out[:, at : at + BLOCK] = jnp.zeros((OBS, BLOCK), F32)
    top = mm(inv, out[at : at + BLOCK, :])
    lane = lax.broadcasted_iota(jnp.int32, (BLOCK, OBS), 1)
    inv_wide = jnp.concatenate([inv] * (OBS // BLOCK), axis=1)
    top = jnp.where((lane >= at) & (lane < at + BLOCK), inv_wide, top)
    out[at : at + BLOCK, :] = top
    out[...] -= mm(column, top)


def inverse_first_body(blocks, noise, out):
    for b in range(BANDS):
        for x in range(BANDS):
            out[x * PER_BAND : (x + 1) * PER_BAND, b * PER_BAND : (b + 1) * PER_BAND] = blocks[
                b * BANDS + x
            ]
    r = lax.broadcasted_iota(jnp.int32, (OBS, OBS), 0)
    c = lax.broadcasted_iota(jnp.int32, (OBS, OBS), 1)
    out[...] += jnp.where(r == c, noise[...], 0.0)
    sweep(out, 0)


def inverse_body(at, before, out):
    out[...] = before[...]
    sweep(out, at)


def stack_body(*refs):
    for j, ref in enumerate(refs[:-1]):
        refs[-1][j * PER_SLAB : (j + 1) * PER_SLAB, :] = ref[...]


def order_body(place, out):
    col = place[1]
    r = lax.broadcasted_iota(jnp.int32, (OBS, OBS), 0)
    n = lax.broadcasted_iota(jnp.int32, (1, OBS), 1)

    def away(j):
        return jnp.where((j & 1) == 1, (j + 1) // 2, -(j // 2))

    core = (n // HALF + col) & 1
    x = (col // 16 + away(n // 48 % 4)) & 3
    z = (col // 2 + away(n // PER_SLAB % 8)) & 7
    out[...] = (r == x * PER_BAND + z * 12 + core * PER_SLAB + n % PER_SLAB).astype(F32)


def update_body(picked, inverse, order, coef, a, north, south, *refs):
    pieces, (out, gain, wide) = refs[:-3], refs[-3:]

    @pl.when(pl.program_id(0) == 0)
    def _():
        for b in range(BANDS):
            wide[:, b * PER_BAND : (b + 1) * PER_BAND] = picked[b]
        gain[...] = mm(mm(wide[...], inverse[...]), order[...])

    rows = jnp.concatenate([piece[...] for piece in pieces], axis=0)
    out[...] = second_step(coef, a[...], north[...], south[...]) - mm(gain[...], rows)


def vmem():
    return pl.BlockSpec(memory_space=pltpu.VMEM)


def smem():
    return pl.BlockSpec(memory_space=pltpu.SMEM)


def shape(*dims):
    return jax.ShapeDtypeStruct(dims, F32)


def split_col(c):
    return c // 16, (c // 2) % 8, c % 2


def move(c, step):
    x, z, k = (a + b for a, b in zip(split_col(c), step))
    return x % 4 * 16 + z % 8 * 2 + k % 2


def col_groups(key):
    groups = {}
    for c in range(SLABS):
        groups.setdefault(key(*split_col(c)), []).append(c)
    return [groups[k] for k in sorted(groups)]


def to_all(shard, axis, count, groups=None):
    return lax.all_to_all(
        jnp.broadcast_to(shard[None], (count, *shard.shape)),
        axis,
        0,
        0,
        tiled=True,
        axis_index_groups=groups,
    )


def local(covariance, wind_east, wind_north, obs_owner, obs_offset, obs_variance):
    band = lax.axis_index("band")
    col = lax.axis_index("col")
    place = jnp.stack([band, col])

    up_band = [(i, i + 1) for i in range(BANDS - 1)]
    down_band = [(i + 1, i) for i in range(BANDS - 1)]
    up_col = [(i, i + 1) for i in range(SLABS - 1)]
    down_col = [(i + 1, i) for i in range(SLABS - 1)]

    def along(value, step):
        pairs = [(c, move(c, step)) for c in range(SLABS)]
        return lax.ppermute(value, "col", pairs)

    below = lax.ppermute(covariance[:, EDGE_START:], "band", up_band)
    above = lax.ppermute(covariance[:, :EDGE], "band", down_band)

    near, index, noise, first_coef, slab_coef, weights = pl.pallas_call(
        prepare_body,
        out_shape=[
            jax.ShapeDtypeStruct((8, BLOCK), jnp.int32),
            jax.ShapeDtypeStruct((1, BLOCK), jnp.int32),
            shape(1, OBS),
            shape(8, ROWS),
            shape(8, LONS),
            shape(8, BLOCK),
        ],
        in_specs=[smem()] + [vmem()] * 5,
        out_specs=[vmem()] * 6,
        name="prepare",
    )(place, obs_owner, obs_offset, obs_variance, wind_east, wind_north)

    advected, for_up, for_down, own = pl.pallas_call(
        first_body,
        out_shape=[shape(LONS, ROWS)] + [shape(16, ROWS)] * 3,
        in_specs=[smem()] + [vmem()] * 6,
        out_specs=[vmem()] * 4,
        scratch_shapes=[pltpu.VMEM((16, ROWS), F32)],
        name="first",
    )(near, weights, covariance, first_coef, below, above, index)

    south_rows = lax.ppermute(for_up, "col", up_col)
    north_rows = lax.ppermute(for_down, "col", down_col)
    south_slab = lax.ppermute(advected, "col", up_col)
    north_slab = lax.ppermute(advected, "col", down_col)

    second_coef = slab_coef.T
    rows, block, picked = pl.pallas_call(
        observed_body,
        out_shape=[shape(PER_SLAB, ROWS), shape(PER_SLAB, PER_BAND), shape(LONS, PER_BAND)],
        in_specs=[vmem()] * 6,
        out_specs=[vmem()] * 3,
        name="observed",
    )(weights, second_coef, own, north_rows, south_rows, index)

    blocks = to_all(block, "col", 16, col_groups(lambda x, z, k: x))
    blocks = blocks.reshape(PER_BAND, PER_BAND)
    blocks = to_all(
        blocks,
        ("band", "col"),
        16,
        [[b * SLABS + x * 16 + low for b in range(BANDS) for x in range(4)] for low in range(16)],
    )
    lines = [rows] + [along(rows, (0, -d, 0)) for d in (1, 7, 2, 6, 3, 5, 4)]
    line = pl.pallas_call(
        stack_body,
        out_shape=shape(48, ROWS),
        in_specs=[vmem()] * 8,
        out_specs=vmem(),
        name="stack",
    )(*lines)
    east, west = along(line, (-1, 0, 0)), along(line, (1, 0, 0))
    far = [along(east[:24], (-1, 0, 0)), along(west[24:], (1, 0, 0))]
    pieces = [line, east, west] + far
    pieces += [along(piece, (0, 0, 1)) for piece in pieces]
    picked_all = to_all(picked, "band", BANDS)

    inverse = pl.pallas_call(
        inverse_first_body,
        out_shape=shape(OBS, OBS),
        in_specs=[vmem()] * 2,
        out_specs=vmem(),
        name="inverse_0",
    )(blocks, noise)
    for step in (1, 2):
        inverse = pl.pallas_call(
            partial(inverse_body, step * BLOCK),
            out_shape=shape(OBS, OBS),
            in_specs=[vmem()],
            out_specs=vmem(),
        )(inverse)

    order = pl.pallas_call(
        order_body,
        out_shape=shape(OBS, OBS),
        in_specs=[smem()],
        out_specs=vmem(),
        name="order",
    )(place)
    chunk = lambda height: pl.BlockSpec((height, CHUNK), lambda i: (0, i))
    return pl.pallas_call(
        update_body,
        out_shape=shape(LONS, ROWS),
        grid=(4,),
        in_specs=[
            pl.BlockSpec((BANDS, LONS, PER_BAND), lambda i: (0, 0, 0)),
            pl.BlockSpec((OBS, OBS), lambda i: (0, 0)),
            pl.BlockSpec((OBS, OBS), lambda i: (0, 0)),
            pl.BlockSpec((LONS, 8), lambda i: (0, 0)),
        ]
        + [chunk(LONS)] * 3
        + [chunk(h) for h in (48, 48, 48, 24, 24)] * 2,
        out_specs=chunk(LONS),
        scratch_shapes=[pltpu.VMEM((LONS, OBS), F32), pltpu.VMEM((LONS, OBS), F32)],
        name="update",
    )(picked_all, inverse, order, second_coef, advected, north_slab, south_slab, *pieces)


def solution(mesh):
    return jax.shard_map(
        local,
        mesh=mesh,
        in_specs=(P("col", "band"), P(), P(), P(), P(), P()),
        out_specs=P("col", "band"),
        check_vma=False,
    )
```

```python
from functools import partial

import jax
import jax.numpy as jnp
from jax import lax
from jax.experimental import pallas as pl
from jax.experimental.pallas import tpu as pltpu
from jax.sharding import PartitionSpec as P


LATS = 64
LONS = 160
BANDS = 4
SLABS = 64
STRIP = LATS // BANDS
ROWS = STRIP * LONS
BATCHES = 3
PER_SLAB = 6
OBS = SLABS * PER_SLAB
PER_BAND = OBS // BANDS
EDGE = 256
EDGE_START = ROWS - EDGE
EDGE_LOW = EDGE - LONS
HALF = OBS // 2
SIDE = ROWS // 2
CHUNK = SIDE // 2
BLOCK = 128
HIGHEST = lax.Precision.HIGHEST
F32 = jnp.float32


def mm(a, b):
    return lax.dot_general(
        a, b, (((1,), (0,)), ((), ())), precision=HIGHEST, preferred_element_type=F32
    )


def pick(a, chosen):
    chosen = chosen.astype(jnp.bfloat16)
    total = None
    for _ in range(3):
        part = a.astype(jnp.bfloat16)
        a = a - part.astype(F32)
        term = lax.dot_general(
            part, chosen, (((1,), (0,)), ((), ())), preferred_element_type=F32
        )
        total = term if total is None else total + term
    return total


def stencil(east, west, north, south):
    here = (
        1.0
        - jnp.maximum(east, 0.0)
        + jnp.minimum(west, 0.0)
        - jnp.maximum(north, 0.0)
        + jnp.minimum(south, 0.0)
    )
    return [
        here,
        -jnp.minimum(east, 0.0),
        jnp.maximum(west, 0.0),
        -jnp.minimum(north, 0.0),
        jnp.maximum(south, 0.0),
    ]


def westward(wind):
    return jnp.concatenate([wind[:, LONS - 1 :], wind[:, : LONS - 1]], axis=1)


def prepare_body(
    place, owner, offset, variance, wind_east, wind_north,
    near_out, index_out, noise_out, first_out, second_out, weights_out,
):
    band, col = place[0], place[1]
    sub = lax.broadcasted_iota(jnp.int32, (BLOCK, BLOCK), 0)
    lane = lax.broadcasted_iota(jnp.int32, (BLOCK, BLOCK), 1)
    target = lax.broadcasted_iota(jnp.int32, (BLOCK, OBS), 1)
    natural = jnp.zeros((1, OBS), jnp.int32)
    offsets = jnp.zeros((1, OBS), jnp.int32)
    noise = jnp.zeros((1, OBS), F32)

    def tall(row):
        return jnp.transpose(jnp.broadcast_to(row, (BLOCK, BLOCK)))

    def wide(v):
        return jnp.concatenate([v] * BATCHES, axis=1)

    for t in range(BATCHES):
        row = owner[t : t + 1, :]
        flat = jnp.broadcast_to(row, (BLOCK, BLOCK))
        same = (flat == jnp.transpose(flat)) & (sub < lane)
        rank = jnp.sum(same.astype(jnp.int32), axis=0, keepdims=True)
        within = 2 * t + rank
        plain = wide(tall(row * PER_SLAB + within)) == target
        lanes = (row // 16) * PER_BAND + (row & 1) * 48 + (row // 2 % 8) * PER_SLAB + within
        hit = wide(tall(lanes)) == target
        away = wide(tall(offset[t : t + 1, :]))
        natural += jnp.sum(jnp.where(plain, away, 0), axis=0, keepdims=True)
        offsets += jnp.sum(jnp.where(hit, away, 0), axis=0, keepdims=True)
        noise += jnp.sum(
            jnp.where(hit, wide(tall(variance[t : t + 1, :])), 0.0), axis=0, keepdims=True
        )
    noise_out[...] = noise
    spread = jnp.broadcast_to(natural, (8, OBS))
    shift = (SLABS + 1 - col) * PER_SLAB
    near = pltpu.roll(spread, lax.rem(shift, OBS), 1)[:, :BLOCK]
    near_out[...] = near
    n = lax.broadcasted_iota(jnp.int32, (8, OBS), 1)
    slab = (n // PER_SLAB % 8) * 2 + n // 48 % 2
    spread = jnp.broadcast_to(offsets, (8, OBS)) + slab * LONS
    points = pltpu.roll(spread, lax.rem(OBS - band * PER_BAND, OBS), 1)[0:1, :BLOCK]
    index_out[...] = jnp.where(lane[0:1, :] < PER_BAND, points, -1)

    start = pl.multiple_of(band * STRIP, STRIP)
    lat = lax.broadcasted_iota(jnp.int32, (STRIP, LONS), 0)
    lon = lax.broadcasted_iota(jnp.int32, (STRIP, LONS), 1)
    east = wind_east[pl.ds(start, STRIP), :]
    north = wind_north[pl.ds(start, STRIP), :]
    before = wind_north[pl.ds(jnp.maximum(band * STRIP - 1, 0), 1), :]
    south = jnp.concatenate([before, north[: STRIP - 1]], axis=0)
    south = jnp.where(lat + start == 0, 0.0, south)
    north = jnp.where(lat + start == LATS - 1, 0.0, north)
    here, to_east, to_west, to_north, to_south = stencil(east, westward(east), north, south)
    kinds = [
        here,
        jnp.where(lon < LONS - 1, to_east, 0.0),
        jnp.where(lon == LONS - 1, to_east, 0.0),
        jnp.where(lon > 0, to_west, 0.0),
        jnp.where(lon == 0, to_west, 0.0),
        jnp.where(lat < STRIP - 1, to_north, 0.0),
        jnp.where(lat > 0, to_south, 0.0),
        jnp.where(lat == 0, to_south, jnp.where(lat == STRIP - 1, to_north, 0.0)),
    ]
    for r in range(STRIP):
        first_out[:, r * LONS : (r + 1) * LONS] = jnp.concatenate(
            [kind[r : r + 1, :] for kind in kinds], axis=0
        )

    east = wind_east[pl.ds(col, 1), :]
    north = wind_north[pl.ds(col, 1), :]
    south = wind_north[pl.ds(jnp.maximum(col - 1, 0), 1), :]
    north = jnp.where(col == LATS - 1, 0.0, north)
    south = jnp.where(col == 0, 0.0, south)
    slab_coef = jnp.concatenate(
        stencil(east, westward(east), north, south) + [jnp.zeros((3, LONS), F32)], axis=0
    )
    second_out[...] = slab_coef
    own = pltpu.roll(near, BLOCK - PER_SLAB, 1)[0:1, :]
    picked = (lax.broadcasted_iota(jnp.int32, (LONS, BLOCK), 0) == own).astype(F32)
    weights = mm(slab_coef, picked)
    weights = jnp.concatenate([weights, jnp.zeros((BLOCK - 8, BLOCK), F32)], axis=0)
    weights_out[...] = jnp.transpose(weights)[:8, :]


def tiles_to_row(v):
    return jnp.concatenate([v[8 * t : 8 * t + 8, :] for t in range(LONS // 8)], axis=1)


def row_to_tiles(v):
    return jnp.concatenate([v[:, BLOCK * t : BLOCK * (t + 1)] for t in range(LONS // 8)], axis=0)


def first_body(
    near_in, weights, c, coef, below, above, index,
    a_out, up_out, down_out, own_out, pair, near, arrived,
):
    fetch = pltpu.make_async_copy(near_in, near, arrived)
    fetch.start()
    for tile in range(LONS // 8):
        rows = slice(8 * tile, 8 * tile + 8)
        q = c[rows, :]
        acc = coef[0:1, :] * q
        acc += coef[1:2, :] * pltpu.roll(q, ROWS - 1, 1)
        acc += coef[2:3, :] * pltpu.roll(q, LONS - 1, 1)
        acc += coef[3:4, :] * pltpu.roll(q, 1, 1)
        acc += coef[4:5, :] * pltpu.roll(q, ROWS - (LONS - 1), 1)
        acc += coef[5:6, :] * pltpu.roll(q, ROWS - LONS, 1)
        acc += coef[6:7, :] * pltpu.roll(q, LONS, 1)
        a_out[rows, :] = acc
        a_out[rows, :EDGE] += coef[7:8, :EDGE] * pltpu.roll(below[rows, :], LONS, 1)
        a_out[rows, EDGE_START:] += coef[7:8, EDGE_START:] * pltpu.roll(above[rows, :], EDGE_LOW, 1)
    fetch.wait()
    up_out[:8, :] = jnp.zeros((8, ROWS), F32)
    down_out[:8, :] = jnp.zeros((8, ROWS), F32)
    own_out[:8, :] = jnp.zeros((8, ROWS), F32)
    pair[...] = jnp.zeros(pair.shape, F32)
    for k in range(PER_SLAB):
        up_out[k : k + 1, :] = a_out[pl.ds(near[0, 2 * PER_SLAB + k], 1), :]
        down_out[k : k + 1, :] = a_out[pl.ds(near[0, k], 1), :]
        o = near[0, PER_SLAB + k]
        own_out[k : k + 1, :] = a_out[pl.ds(o, 1), :]
        pair[k : k + 1, :] = a_out[pl.ds(jnp.where(o == LONS - 1, 0, o + 1), 1), :]
        pair[k + 8 : k + 9, :] = a_out[pl.ds(jnp.where(o == 0, LONS - 1, o - 1), 1), :]
    own_out[:8, :] = (
        weights[:, 0:1] * own_out[:8, :]
        + weights[:, 1:2] * pair[:8, :]
        + weights[:, 2:3] * pair[8:, :]
    )
    width = ROWS // 5
    total = jnp.zeros((LONS, BLOCK), F32)
    for part in range(5):
        lanes = lax.broadcasted_iota(jnp.int32, (width, BLOCK), 0) + part * width
        total += pick(a_out[:, part * width : (part + 1) * width], lanes == index[...])
    packed = tiles_to_row(total)
    for ref in (up_out, down_out, own_out):
        ref[8:, :] = packed


def observed_body(weights, coef, own, north, south, index, rows_out, picked_out):
    rows = own[:8, :] + weights[:, 3:4] * north[:8, :] + weights[:, 4:5] * south[:8, :]
    rows_out[:, :ROWS] = rows[:PER_SLAB, :]
    width = ROWS // 5
    total = jnp.zeros((8, BLOCK), F32)
    for part in range(5):
        lanes = lax.broadcasted_iota(jnp.int32, (width, BLOCK), 0) + part * width
        total += pick(rows[:, part * width : (part + 1) * width], lanes == index[...])
    rows_out[:, ROWS:] = total[:PER_SLAB, :]
    q = row_to_tiles(own[8:, :])
    picked = second_step(coef, q, row_to_tiles(north[8:, :]), row_to_tiles(south[8:, :]))
    picked_out[...] = picked[:, :PER_BAND]


def second_step(coef, q, north, south):
    return (
        coef[:, 0:1] * q
        + coef[:, 1:2] * pltpu.roll(q, LONS - 1, 0)
        + coef[:, 2:3] * pltpu.roll(q, 1, 0)
        + coef[:, 3:4] * north
        + coef[:, 4:5] * south
    )


def inverse_2(a, b, d):
    scale = 1.0 / (a * d - b * b)
    return d * scale, -b * scale, a * scale


def inverse_block(m):
    n = BLOCK
    lane = lax.broadcasted_iota(jnp.int32, (8, n), 1)
    sub = lax.broadcasted_iota(jnp.int32, (8, n), 0)
    tiles = [m[8 * t : 8 * t + 8, :] for t in range(n // 8)]
    for j in range(0, n, 4):
        home, base = j // 8, j % 8
        columns = [
            [
                jnp.take_along_axis(tile, jnp.full((8, n), j + k, jnp.int32), axis=1)
                for k in range(4)
            ]
            for tile in tiles
        ]
        p = [
            [
                jnp.broadcast_to(columns[home][k][base + i : base + i + 1, :], (8, n))
                for k in range(4)
            ]
            for i in range(4)
        ]
        a00, a01, a11 = inverse_2(p[0][0], p[0][1], p[1][1])
        y00 = a00 * p[0][2] + a01 * p[1][2]
        y01 = a00 * p[0][3] + a01 * p[1][3]
        y10 = a01 * p[0][2] + a11 * p[1][2]
        y11 = a01 * p[0][3] + a11 * p[1][3]
        s00 = p[2][2] - (p[0][2] * y00 + p[1][2] * y10)
        s01 = p[2][3] - (p[0][2] * y01 + p[1][2] * y11)
        s11 = p[3][3] - (p[0][3] * y01 + p[1][3] * y11)
        d00, d01, d11 = inverse_2(s00, s01, s11)
        z00 = y00 * d00 + y01 * d01
        z01 = y00 * d01 + y01 * d11
        z10 = y10 * d00 + y11 * d01
        z11 = y10 * d01 + y11 * d11
        b00 = a00 + z00 * y00 + z01 * y01
        b01 = a01 + z00 * y10 + z01 * y11
        b11 = a11 + z10 * y10 + z11 * y11
        inv = [
            [b00, b01, -z00, -z01],
            [b01, b11, -z10, -z11],
            [-z00, -z10, d00, d01],
            [-z01, -z11, d01, d11],
        ]
        rows = [
            jnp.where(
                (lane >= j) & (lane < j + 4),
                jnp.where(lane == j + i, 1.0, 0.0),
                jnp.broadcast_to(tiles[home][base + i : base + i + 1, :], (8, n)),
            )
            for i in range(4)
        ]
        t = [
            (inv[i][0] * rows[0] + inv[i][1] * rows[1]) + (inv[i][2] * rows[2] + inv[i][3] * rows[3])
            for i in range(4)
        ]
        swept = []
        for number, tile in enumerate(tiles):
            col = columns[number]
            kept = jnp.where((lane >= j) & (lane < j + 4), 0.0, tile)
            new = kept - ((col[0] * t[0] + col[1] * t[1]) + (col[2] * t[2] + col[3] * t[3]))
            if number == home:
                for i in range(4):
                    new = jnp.where(sub == base + i, t[i], new)
            swept.append(new)
        tiles = swept
    return jnp.concatenate(tiles, axis=0)


def sweep(out, at):
    inv = inverse_block(out[at : at + BLOCK, at : at + BLOCK])
    row_id = lax.broadcasted_iota(jnp.int32, (OBS, BLOCK), 0)
    column = out[:, at : at + BLOCK]
    column = jnp.where((row_id >= at) & (row_id < at + BLOCK), 0.0, column)
    out[:, at : at + BLOCK] = jnp.zeros((OBS, BLOCK), F32)
    top = mm(inv, out[at : at + BLOCK, :])
    lane = lax.broadcasted_iota(jnp.int32, (BLOCK, OBS), 1)
    inv_wide = jnp.concatenate([inv] * (OBS // BLOCK), axis=1)
    top = jnp.where((lane >= at) & (lane < at + BLOCK), inv_wide, top)
    out[at : at + BLOCK, :] = top
    out[...] -= mm(column, top)


def inverse_first_body(blocks, noise, out):
    for b in range(BANDS):
        for part in range(8):
            out[part * 48 : part * 48 + 48, b * PER_BAND : (b + 1) * PER_BAND] = blocks[
                b * 8 + part
            ]
    r = lax.broadcasted_iota(jnp.int32, (OBS, OBS), 0)
    c = lax.broadcasted_iota(jnp.int32, (OBS, OBS), 1)
    out[...] += jnp.where(r == c, noise[...], 0.0)
    sweep(out, 0)


def inverse_body(at, before, out):
    out[...] = before[...]
    sweep(out, at)


def triple_body(own, above, below, three_out, two_out):
    rows = jnp.concatenate([own[...], above[...], below[...]], axis=0)
    three_out[...] = rows
    two_out[...] = rows[:12, :]


Z_AWAY = (0, 1, -1, 3, 4, 2, -3, -2)
X_AWAY = (0, 1, -1, 2)


def away(j, steps):
    return sum(jnp.where(j == i, step, 0) for i, step in enumerate(steps))


def stack_body(place, near, above, below, line_out, block_out):
    rows = jnp.concatenate([near[...], above[...], below[...]], axis=0)
    line_out[...] = rows[:, :ROWS]
    n = lax.broadcasted_iota(jnp.int32, (48, 48), 1)
    r = lax.broadcasted_iota(jnp.int32, (48, 48), 0)
    z = (place[1] // 2 + away(n // PER_SLAB, Z_AWAY)) & 7
    sort = (r == z * PER_SLAB + n % PER_SLAB).astype(F32)
    block_out[...] = mm(sort, rows[:, ROWS:])[:, :PER_BAND]


def order_body(place, out):
    col = place[1]
    r = lax.broadcasted_iota(jnp.int32, (OBS, OBS), 0)
    n = lax.broadcasted_iota(jnp.int32, (1, OBS), 1)
    core = (n // HALF + col) & 1
    x = (col // 16 + away(n // 48 % 4, X_AWAY)) & 3
    z = (col // 2 + away(n // PER_SLAB % 8, Z_AWAY)) & 7
    out[...] = (r == x * PER_BAND + core * 48 + z * PER_SLAB + n % PER_SLAB).astype(F32)


def update_body(picked, inverse, order, coef, a, north, south, *refs):
    pieces, (out, gain, wide) = refs[:-3], refs[-3:]

    @pl.when(pl.program_id(0) == 0)
    def _():
        for b in range(BANDS):
            wide[:, b * PER_BAND : (b + 1) * PER_BAND] = picked[b]
        gain[...] = mm(mm(wide[...], inverse[...]), order[...])

    rows = jnp.concatenate([piece[...] for piece in pieces], axis=0)
    out[...] = second_step(coef, a[...], north[...], south[...]) - mm(gain[...], rows)


def vmem():
    return pl.BlockSpec(memory_space=pltpu.VMEM)


def smem():
    return pl.BlockSpec(memory_space=pltpu.SMEM)


def shape(*dims):
    return jax.ShapeDtypeStruct(dims, F32)


def split_col(c):
    return c // 16, (c // 2) % 8, c % 2


def move(c, step):
    x, z, k = (a + b for a, b in zip(split_col(c), step))
    return x % 4 * 16 + z % 8 * 2 + k % 2


def to_all(shard, axis, count, groups=None):
    return lax.all_to_all(
        jnp.broadcast_to(shard[None], (count, *shard.shape)),
        axis,
        0,
        0,
        tiled=True,
        axis_index_groups=groups,
    )


def local(covariance, wind_east, wind_north, obs_owner, obs_offset, obs_variance):
    band = lax.axis_index("band")
    col = lax.axis_index("col")
    place = jnp.stack([band, col])

    up_band = [(i, i + 1) for i in range(BANDS - 1)]
    down_band = [(i + 1, i) for i in range(BANDS - 1)]
    up_col = [(i, i + 1) for i in range(SLABS - 1)]
    down_col = [(i + 1, i) for i in range(SLABS - 1)]

    def along(value, step):
        pairs = [(c, move(c, step)) for c in range(SLABS)]
        return lax.ppermute(value, "col", pairs)

    below = lax.ppermute(covariance[:, EDGE_START:], "band", up_band)
    above = lax.ppermute(covariance[:, :EDGE], "band", down_band)

    near, index, noise, first_coef, slab_coef, weights = pl.pallas_call(
        prepare_body,
        out_shape=[
            jax.ShapeDtypeStruct((8, BLOCK), jnp.int32),
            jax.ShapeDtypeStruct((1, BLOCK), jnp.int32),
            shape(1, OBS),
            shape(8, ROWS),
            shape(8, LONS),
            shape(8, BLOCK),
        ],
        in_specs=[smem()] + [vmem()] * 5,
        out_specs=[vmem()] * 6,
        name="prepare",
    )(place, obs_owner, obs_offset, obs_variance, wind_east, wind_north)

    advected, for_up, for_down, own = pl.pallas_call(
        first_body,
        out_shape=[shape(LONS, ROWS)] + [shape(16, ROWS)] * 3,
        in_specs=[vmem()] * 7,
        out_specs=[vmem()] * 4,
        scratch_shapes=[
            pltpu.VMEM((16, ROWS), F32),
            pltpu.SMEM((8, BLOCK), jnp.int32),
            pltpu.SemaphoreType.DMA,
        ],
        name="first",
    )(near, weights, covariance, first_coef, below, above, index)

    south_rows = lax.ppermute(for_up, "col", up_col)
    north_rows = lax.ppermute(for_down, "col", down_col)
    south_slab = lax.ppermute(advected, "col", up_col)
    north_slab = lax.ppermute(advected, "col", down_col)

    second_coef = slab_coef.T
    rows, picked = pl.pallas_call(
        observed_body,
        out_shape=[shape(PER_SLAB, ROWS + BLOCK), shape(LONS, PER_BAND)],
        in_specs=[vmem()] * 6,
        out_specs=[vmem()] * 2,
        name="observed",
    )(weights, second_coef, own, north_rows, south_rows, index)

    three, two = pl.pallas_call(
        triple_body,
        out_shape=[shape(18, ROWS + BLOCK), shape(12, ROWS + BLOCK)],
        in_specs=[vmem()] * 3,
        out_specs=[vmem()] * 2,
        name="triple",
    )(rows, along(rows, (0, -1, 0)), along(rows, (0, 1, 0)))
    picked_all = to_all(picked, "band", BANDS)
    line, block = pl.pallas_call(
        stack_body,
        out_shape=[shape(48, ROWS), shape(48, PER_BAND)],
        in_specs=[smem()] + [vmem()] * 3,
        out_specs=[vmem()] * 2,
        name="stack",
    )(place, three, along(three, (0, -3, 0)), along(two, (0, 3, 0)))
    blocks = to_all(
        block,
        ("band", "col"),
        32,
        [
            [
                b * SLABS + x * 16 + z * 2 + k
                for b in range(BANDS)
                for x in range(4)
                for k in range(2)
            ]
            for z in range(8)
        ],
    )
    east, west = along(line, (-1, 0, 0)), along(line, (1, 0, 0))
    far = [along(east[:24], (-1, 0, 0)), along(west[24:], (1, 0, 0))]
    pieces = [line, east, west] + far
    pieces += [along(piece, (0, 0, 1)) for piece in pieces]

    inverse = pl.pallas_call(
        inverse_first_body,
        out_shape=shape(OBS, OBS),
        in_specs=[vmem()] * 2,
        out_specs=vmem(),
        name="inverse_0",
    )(blocks, noise)
    for step in (1, 2):
        inverse = pl.pallas_call(
            partial(inverse_body, step * BLOCK),
            out_shape=shape(OBS, OBS),
            in_specs=[vmem()],
            out_specs=vmem(),
        )(inverse)

    order = pl.pallas_call(
        order_body,
        out_shape=shape(OBS, OBS),
        in_specs=[smem()],
        out_specs=vmem(),
        name="order",
    )(place)
    chunk = lambda height: pl.BlockSpec((height, CHUNK), lambda i: (0, i))
    return pl.pallas_call(
        update_body,
        out_shape=shape(LONS, ROWS),
        grid=(4,),
        in_specs=[
            pl.BlockSpec((BANDS, LONS, PER_BAND), lambda i: (0, 0, 0)),
            pl.BlockSpec((OBS, OBS), lambda i: (0, 0)),
            pl.BlockSpec((OBS, OBS), lambda i: (0, 0)),
            pl.BlockSpec((LONS, 8), lambda i: (0, 0)),
        ]
        + [chunk(LONS)] * 3
        + [chunk(h) for h in (48, 48, 48, 24, 24)] * 2,
        out_specs=chunk(LONS),
        scratch_shapes=[pltpu.VMEM((LONS, OBS), F32), pltpu.VMEM((LONS, OBS), F32)],
        name="update",
    )(picked_all, inverse, order, second_coef, advected, north_slab, south_slab, *pieces)


def solution(mesh):
    return jax.shard_map(
        local,
        mesh=mesh,
        in_specs=(P("col", "band"), P(), P(), P(), P(), P()),
        out_specs=P("col", "band"),
        check_vma=False,
    )
```

```python
from functools import partial

import jax
import jax.numpy as jnp
from jax import lax
from jax.experimental import pallas as pl
from jax.experimental.pallas import tpu as pltpu
from jax.sharding import PartitionSpec as P


LATS = 64
LONS = 160
BANDS = 4
SLABS = 64
STRIP = LATS // BANDS
ROWS = STRIP * LONS
BATCHES = 3
PER_SLAB = 6
OBS = SLABS * PER_SLAB
PER_BAND = OBS // BANDS
EDGE = 256
EDGE_START = ROWS - EDGE
EDGE_LOW = EDGE - LONS
HALF = OBS // 2
SIDE = ROWS // 2
CHUNK = SIDE // 2
BLOCK = 128
HIGHEST = lax.Precision.HIGHEST
F32 = jnp.float32


def mm(a, b):
    return lax.dot_general(
        a, b, (((1,), (0,)), ((), ())), precision=HIGHEST, preferred_element_type=F32
    )


def pick(a, chosen):
    chosen = chosen.astype(jnp.bfloat16)
    total = None
    for _ in range(3):
        part = a.astype(jnp.bfloat16)
        a = a - part.astype(F32)
        term = lax.dot_general(
            part, chosen, (((1,), (0,)), ((), ())), preferred_element_type=F32
        )
        total = term if total is None else total + term
    return total


def stencil(east, west, north, south):
    here = (
        1.0
        - jnp.maximum(east, 0.0)
        + jnp.minimum(west, 0.0)
        - jnp.maximum(north, 0.0)
        + jnp.minimum(south, 0.0)
    )
    return [
        here,
        -jnp.minimum(east, 0.0),
        jnp.maximum(west, 0.0),
        -jnp.minimum(north, 0.0),
        jnp.maximum(south, 0.0),
    ]


def westward(wind):
    return jnp.concatenate([wind[:, LONS - 1 :], wind[:, : LONS - 1]], axis=1)


def prepare_body(
    owner, offset, variance, wind_east, wind_north,
    near_out, index_out, noise_out, first_out, second_out, weights_out,
):
    band, col = lax.axis_index("band"), lax.axis_index("col")
    sub = lax.broadcasted_iota(jnp.int32, (BLOCK, BLOCK), 0)
    lane = lax.broadcasted_iota(jnp.int32, (BLOCK, BLOCK), 1)
    target = lax.broadcasted_iota(jnp.int32, (BLOCK, OBS), 1)
    natural = jnp.zeros((1, OBS), jnp.int32)
    offsets = jnp.zeros((1, OBS), jnp.int32)
    noise = jnp.zeros((1, OBS), F32)

    def tall(row):
        return jnp.transpose(jnp.broadcast_to(row, (BLOCK, BLOCK)))

    def wide(v):
        return jnp.concatenate([v] * BATCHES, axis=1)

    for t in range(BATCHES):
        row = owner[t : t + 1, :]
        flat = jnp.broadcast_to(row, (BLOCK, BLOCK))
        same = (flat == jnp.transpose(flat)) & (sub < lane)
        rank = jnp.sum(same.astype(jnp.int32), axis=0, keepdims=True)
        within = 2 * t + rank
        plain = wide(tall(row * PER_SLAB + within)) == target
        lanes = (row // 16) * PER_BAND + (row & 1) * 48 + (row // 2 % 8) * PER_SLAB + within
        hit = wide(tall(lanes)) == target
        away = wide(tall(offset[t : t + 1, :]))
        natural += jnp.sum(jnp.where(plain, away, 0), axis=0, keepdims=True)
        offsets += jnp.sum(jnp.where(hit, away, 0), axis=0, keepdims=True)
        noise += jnp.sum(
            jnp.where(hit, wide(tall(variance[t : t + 1, :])), 0.0), axis=0, keepdims=True
        )
    noise_out[...] = noise
    spread = jnp.broadcast_to(natural, (8, OBS))
    shift = (SLABS + 1 - col) * PER_SLAB
    near = pltpu.roll(spread, lax.rem(shift, OBS), 1)[:, :BLOCK]
    near_out[...] = near
    n = lax.broadcasted_iota(jnp.int32, (8, OBS), 1)
    slab = (n // PER_SLAB % 8) * 2 + n // 48 % 2
    spread = jnp.broadcast_to(offsets, (8, OBS)) + slab * LONS
    points = pltpu.roll(spread, lax.rem(OBS - band * PER_BAND, OBS), 1)[0:1, :BLOCK]
    index_out[...] = jnp.where(lane[0:1, :] < PER_BAND, points, -1)

    start = pl.multiple_of(band * STRIP, STRIP)
    lat = lax.broadcasted_iota(jnp.int32, (STRIP, LONS), 0)
    lon = lax.broadcasted_iota(jnp.int32, (STRIP, LONS), 1)
    east = wind_east[pl.ds(start, STRIP), :]
    north = wind_north[pl.ds(start, STRIP), :]
    before = wind_north[pl.ds(jnp.maximum(band * STRIP - 1, 0), 1), :]
    south = jnp.concatenate([before, north[: STRIP - 1]], axis=0)
    south = jnp.where(lat + start == 0, 0.0, south)
    north = jnp.where(lat + start == LATS - 1, 0.0, north)
    here, to_east, to_west, to_north, to_south = stencil(east, westward(east), north, south)
    kinds = [
        here,
        jnp.where(lon < LONS - 1, to_east, 0.0),
        jnp.where(lon == LONS - 1, to_east, 0.0),
        jnp.where(lon > 0, to_west, 0.0),
        jnp.where(lon == 0, to_west, 0.0),
        jnp.where(lat < STRIP - 1, to_north, 0.0),
        jnp.where(lat > 0, to_south, 0.0),
        jnp.where(lat == 0, to_south, jnp.where(lat == STRIP - 1, to_north, 0.0)),
    ]
    for r in range(STRIP):
        first_out[:, r * LONS : (r + 1) * LONS] = jnp.concatenate(
            [kind[r : r + 1, :] for kind in kinds], axis=0
        )
    flat = first_out[...]
    kind = lax.broadcasted_iota(jnp.int32, (8, ROWS), 0)
    ahead = (kind == 1) | (kind == 2)
    behind = (kind == 3) | (kind == 4)
    first_out[...] = jnp.where(
        ahead, pltpu.roll(flat, 1, 1), jnp.where(behind, pltpu.roll(flat, ROWS - 1, 1), flat)
    )

    east = wind_east[pl.ds(col, 1), :]
    north = wind_north[pl.ds(col, 1), :]
    south = wind_north[pl.ds(jnp.maximum(col - 1, 0), 1), :]
    north = jnp.where(col == LATS - 1, 0.0, north)
    south = jnp.where(col == 0, 0.0, south)
    slab_coef = jnp.concatenate(
        stencil(east, westward(east), north, south) + [jnp.zeros((3, LONS), F32)], axis=0
    )
    second_out[...] = slab_coef
    own = pltpu.roll(near, BLOCK - PER_SLAB, 1)[0:1, :]
    picked = (lax.broadcasted_iota(jnp.int32, (LONS, BLOCK), 0) == own).astype(F32)
    weights = mm(slab_coef, picked)
    weights = jnp.concatenate([weights, jnp.zeros((BLOCK - 8, BLOCK), F32)], axis=0)
    weights_out[...] = jnp.transpose(weights)[:8, :]


def tiles_to_row(v):
    return jnp.concatenate([v[8 * t : 8 * t + 8, :] for t in range(LONS // 8)], axis=1)


def row_to_tiles(v):
    return jnp.concatenate([v[:, BLOCK * t : BLOCK * (t + 1)] for t in range(LONS // 8)], axis=0)


def first_body(
    near_in, weights, c, coef, below, above, index,
    a_out, up_out, down_out, own_out, pair, near, arrived,
):
    fetch = pltpu.make_async_copy(near_in, near, arrived)
    fetch.start()
    for tile in range(LONS // 8):
        rows = slice(8 * tile, 8 * tile + 8)
        q = c[rows, :]
        north, south = pltpu.roll(q, ROWS - LONS, 1), pltpu.roll(q, LONS, 1)
        acc = coef[0:1, :] * q + coef[5:6, :] * north + coef[6:7, :] * south
        acc += pltpu.roll(coef[1:2, :] * q + coef[2:3, :] * south, ROWS - 1, 1)
        acc += pltpu.roll(coef[3:4, :] * q + coef[4:5, :] * north, 1, 1)
        a_out[rows, :] = acc
        a_out[rows, :EDGE] += coef[7:8, :EDGE] * pltpu.roll(below[rows, :], LONS, 1)
        a_out[rows, EDGE_START:] += coef[7:8, EDGE_START:] * pltpu.roll(above[rows, :], EDGE_LOW, 1)
    fetch.wait()
    up_out[:8, :] = jnp.zeros((8, ROWS), F32)
    down_out[:8, :] = jnp.zeros((8, ROWS), F32)
    own_out[:8, :] = jnp.zeros((8, ROWS), F32)
    pair[...] = jnp.zeros(pair.shape, F32)
    for k in range(PER_SLAB):
        up_out[k : k + 1, :] = a_out[pl.ds(near[0, 2 * PER_SLAB + k], 1), :]
        down_out[k : k + 1, :] = a_out[pl.ds(near[0, k], 1), :]
        o = near[0, PER_SLAB + k]
        own_out[k : k + 1, :] = a_out[pl.ds(o, 1), :]
        pair[k : k + 1, :] = a_out[pl.ds(jnp.where(o == LONS - 1, 0, o + 1), 1), :]
        pair[k + 8 : k + 9, :] = a_out[pl.ds(jnp.where(o == 0, LONS - 1, o - 1), 1), :]
    own_out[:8, :] = (
        weights[:, 0:1] * own_out[:8, :]
        + weights[:, 1:2] * pair[:8, :]
        + weights[:, 2:3] * pair[8:, :]
    )
    width = ROWS // 5
    total = jnp.zeros((LONS, BLOCK), F32)
    for part in range(5):
        lanes = lax.broadcasted_iota(jnp.int32, (width, BLOCK), 0) + part * width
        total += pick(a_out[:, part * width : (part + 1) * width], lanes == index[...])
    packed = tiles_to_row(total)
    for ref in (up_out, down_out, own_out):
        ref[8:, :] = packed


def observed_body(weights, coef, own, north, south, index, rows_out, picked_out):
    rows = own[:8, :] + weights[:, 3:4] * north[:8, :] + weights[:, 4:5] * south[:8, :]
    rows_out[:, :ROWS] = rows[:PER_SLAB, :]
    width = ROWS // 5
    total = jnp.zeros((8, BLOCK), F32)
    for part in range(5):
        lanes = lax.broadcasted_iota(jnp.int32, (width, BLOCK), 0) + part * width
        total += pick(rows[:, part * width : (part + 1) * width], lanes == index[...])
    rows_out[:, ROWS:] = total[:PER_SLAB, :]
    q = row_to_tiles(own[8:, :])
    picked = second_step(coef, q, row_to_tiles(north[8:, :]), row_to_tiles(south[8:, :]))
    for band in range(BANDS):
        picked_out[band] = picked[:, :PER_BAND]


def second_step(coef, q, north, south):
    return (
        coef[:, 0:1] * q
        + coef[:, 1:2] * pltpu.roll(q, LONS - 1, 0)
        + coef[:, 2:3] * pltpu.roll(q, 1, 0)
        + coef[:, 3:4] * north
        + coef[:, 4:5] * south
    )


def inverse_2(a, b, d):
    scale = 1.0 / (a * d - b * b)
    return d * scale, -b * scale, a * scale


def dots(left, right):
    terms = [l * r for l, r in zip(left, right)]
    while len(terms) > 1:
        odd = terms[len(terms) // 2 * 2 :]
        terms = [u + v for u, v in zip(terms[::2], terms[1::2])] + odd
    return terms[0]


def inverse_4(p):
    a00, a01, a11 = inverse_2(p[0][0], p[0][1], p[1][1])
    y00 = a00 * p[0][2] + a01 * p[1][2]
    y01 = a00 * p[0][3] + a01 * p[1][3]
    y10 = a01 * p[0][2] + a11 * p[1][2]
    y11 = a01 * p[0][3] + a11 * p[1][3]
    s00 = p[2][2] - (p[0][2] * y00 + p[1][2] * y10)
    s01 = p[2][3] - (p[0][2] * y01 + p[1][2] * y11)
    s11 = p[3][3] - (p[0][3] * y01 + p[1][3] * y11)
    d00, d01, d11 = inverse_2(s00, s01, s11)
    z00 = y00 * d00 + y01 * d01
    z01 = y00 * d01 + y01 * d11
    z10 = y10 * d00 + y11 * d01
    z11 = y10 * d01 + y11 * d11
    b00 = a00 + (z00 * y00 + z01 * y01)
    b01 = a01 + (z00 * y10 + z01 * y11)
    b11 = a11 + (z10 * y10 + z11 * y11)
    return [
        [b00, b01, -z00, -z01],
        [b01, b11, -z10, -z11],
        [-z00, -z10, d00, d01],
        [-z01, -z11, d01, d11],
    ]


def inverse_block(m):
    n = BLOCK
    lane = lax.broadcasted_iota(jnp.int32, (8, n), 1)
    sub = lax.broadcasted_iota(jnp.int32, (8, n), 0)
    tiles = [m[8 * t : 8 * t + 8, :] for t in range(n // 8)]
    half = range(4)
    for home in range(n // 8):
        j = 8 * home
        inside = (lane >= j) & (lane < j + 8)
        order = [home] + [t for t in range(n // 8) if t != home]
        order = order[:1] + [t for t in order if t == home + 1] + [t for t in order[1:] if t != home + 1]
        columns = {}
        for t in order:
            columns[t] = [
                jnp.take_along_axis(tiles[t], jnp.full((8, n), j + k, jnp.int32), axis=1)
                for k in range(8)
            ]
        p = [
            [
                jnp.broadcast_to(columns[home][max(i, k)][min(i, k) : min(i, k) + 1, :], (8, n))
                for k in range(8)
            ]
            for i in range(8)
        ]
        p12 = [p[i][4:] for i in half]
        first = inverse_4([p[i][:4] for i in half])
        y = [[dots(first[i], [p12[k][q] for k in half]) for q in half] for i in half]
        schur = [[None] * 4 for _ in half]
        for i in half:
            for q in range(i, 4):
                schur[i][q] = p[4 + i][4 + q] - dots(
                    [p12[k][i] for k in half], [y[k][q] for k in half]
                )
                schur[q][i] = schur[i][q]
        second = inverse_4(schur)
        rows = [
            jnp.where(
                inside,
                jnp.where(lane == j + i, 1.0, 0.0),
                jnp.broadcast_to(tiles[home][i : i + 1, :], (8, n)),
            )
            for i in range(8)
        ]
        top = [dots(first[i], rows[:4]) for i in half]
        low = [rows[4 + i] - dots([p12[k][i] for k in half], top) for i in half]
        low = [dots(second[i], low) for i in half]
        top = [top[i] - dots(y[i], low) for i in half]
        t = top + low
        swept = []
        for number, tile in enumerate(tiles):
            if number == home:
                new = t[0]
                for i in range(1, 8):
                    new = jnp.where(sub == i, t[i], new)
            else:
                new = jnp.where(inside, 0.0, tile) - dots(columns[number], t)
            swept.append(new)
        tiles = swept
    return jnp.concatenate(tiles, axis=0)


def sweep(out, at):
    inv = inverse_block(out[at : at + BLOCK, at : at + BLOCK])
    row_id = lax.broadcasted_iota(jnp.int32, (OBS, BLOCK), 0)
    column = out[:, at : at + BLOCK]
    column = jnp.where((row_id >= at) & (row_id < at + BLOCK), 0.0, column)
    out[:, at : at + BLOCK] = jnp.zeros((OBS, BLOCK), F32)
    top = mm(inv, out[at : at + BLOCK, :])
    lane = lax.broadcasted_iota(jnp.int32, (BLOCK, OBS), 1)
    inv_wide = jnp.concatenate([inv] * (OBS // BLOCK), axis=1)
    top = jnp.where((lane >= at) & (lane < at + BLOCK), inv_wide, top)
    out[at : at + BLOCK, :] = top
    out[...] -= mm(column, top)


def inverse_first_body(blocks, noise, out):
    for b in range(BANDS):
        for part in range(8):
            out[part * 48 : part * 48 + 48, b * PER_BAND : (b + 1) * PER_BAND] = blocks[
                b * 8 + part
            ]
    r = lax.broadcasted_iota(jnp.int32, (OBS, OBS), 0)
    c = lax.broadcasted_iota(jnp.int32, (OBS, OBS), 1)
    out[...] += jnp.where(r == c, noise[...], 0.0)
    sweep(out, 0)


def inverse_body(at, before, out):
    out[...] = before[...]
    sweep(out, at)


def triple_body(own, above, below, three_out, two_out):
    rows = jnp.concatenate([own[...], above[...], below[...]], axis=0)
    three_out[...] = rows
    two_out[...] = rows[:12, :]


Z_AWAY = (0, 1, -1, 3, 4, 2, -3, -2)
X_AWAY = (0, 1, -1, 2)


def away(j, steps):
    return sum(jnp.where(j == i, step, 0) for i, step in enumerate(steps))


def stack_body(near, above, below, line_out, block_out):
    rows = jnp.concatenate([near[...], above[...], below[...]], axis=0)
    line_out[...] = rows[:, :ROWS]
    n = lax.broadcasted_iota(jnp.int32, (48, 48), 1)
    r = lax.broadcasted_iota(jnp.int32, (48, 48), 0)
    z = (lax.axis_index("col") // 2 + away(n // PER_SLAB, Z_AWAY)) & 7
    sort = (r == z * PER_SLAB + n % PER_SLAB).astype(F32)
    block = mm(sort, rows[:, ROWS:])[:, :PER_BAND]
    for copy in range(BANDS * 8):
        block_out[copy] = block


def order_body(out):
    col = lax.axis_index("col")
    r = lax.broadcasted_iota(jnp.int32, (OBS, OBS), 0)
    n = lax.broadcasted_iota(jnp.int32, (1, OBS), 1)
    core = (n // HALF + col) & 1
    x = (col // 16 + away(n // 48 % 4, X_AWAY)) & 3
    z = (col // 2 + away(n // PER_SLAB % 8, Z_AWAY)) & 7
    out[...] = (r == x * PER_BAND + core * 48 + z * PER_SLAB + n % PER_SLAB).astype(F32)


def parts(v):
    high = v.astype(jnp.bfloat16)
    return high, (v - high.astype(F32)).astype(jnp.bfloat16)


def mm_3(a, b):
    a_high, a_low = parts(a)
    b_high, b_low = parts(b)
    dot = lambda u, v: lax.dot_general(
        u, v, (((1,), (0,)), ((), ())), preferred_element_type=F32
    )
    return dot(a_high, b_high) + (dot(a_high, b_low) + dot(a_low, b_high))


def update_body(picked, inverse, order, coef, a, north, south, *refs):
    pieces, (out, gain, wide) = refs[:-3], refs[-3:]

    @pl.when(pl.program_id(0) == 0)
    def _():
        for b in range(BANDS):
            wide[:, b * PER_BAND : (b + 1) * PER_BAND] = picked[b]
        gain[...] = mm(mm(wide[...], inverse[...]), order[...])

    rows = jnp.concatenate([piece[...] for piece in pieces], axis=0)
    out[...] = second_step(coef, a[...], north[...], south[...]) - mm_3(gain[...], rows)


def vmem():
    return pl.BlockSpec(memory_space=pltpu.VMEM)


def shape(*dims):
    return jax.ShapeDtypeStruct(dims, F32)


def split_col(c):
    return c // 16, (c // 2) % 8, c % 2


def move(c, step):
    x, z, k = (a + b for a, b in zip(split_col(c), step))
    return x % 4 * 16 + z % 8 * 2 + k % 2


def to_all(copies, axis, groups=None):
    return lax.all_to_all(copies, axis, 0, 0, tiled=True, axis_index_groups=groups)


def local(covariance, wind_east, wind_north, obs_owner, obs_offset, obs_variance):
    up_band = [(i, i + 1) for i in range(BANDS - 1)]
    down_band = [(i + 1, i) for i in range(BANDS - 1)]
    up_col = [(i, i + 1) for i in range(SLABS - 1)]
    down_col = [(i + 1, i) for i in range(SLABS - 1)]

    def along(value, step):
        pairs = [(c, move(c, step)) for c in range(SLABS)]
        return lax.ppermute(value, "col", pairs)

    below = lax.ppermute(covariance[:, EDGE_START:], "band", up_band)
    above = lax.ppermute(covariance[:, :EDGE], "band", down_band)

    near, index, noise, first_coef, slab_coef, weights = pl.pallas_call(
        prepare_body,
        out_shape=[
            jax.ShapeDtypeStruct((8, BLOCK), jnp.int32),
            jax.ShapeDtypeStruct((1, BLOCK), jnp.int32),
            shape(1, OBS),
            shape(8, ROWS),
            shape(8, LONS),
            shape(8, BLOCK),
        ],
        in_specs=[vmem()] * 5,
        out_specs=[vmem()] * 6,
        name="prepare",
    )(obs_owner, obs_offset, obs_variance, wind_east, wind_north)

    advected, for_up, for_down, own = pl.pallas_call(
        first_body,
        out_shape=[shape(LONS, ROWS)] + [shape(16, ROWS)] * 3,
        in_specs=[vmem()] * 7,
        out_specs=[vmem()] * 4,
        scratch_shapes=[
            pltpu.VMEM((16, ROWS), F32),
            pltpu.SMEM((8, BLOCK), jnp.int32),
            pltpu.SemaphoreType.DMA,
        ],
        name="first",
    )(near, weights, covariance, first_coef, below, above, index)

    south_rows = lax.ppermute(for_up, "col", up_col)
    north_rows = lax.ppermute(for_down, "col", down_col)
    south_slab = lax.ppermute(advected, "col", up_col)
    north_slab = lax.ppermute(advected, "col", down_col)

    second_coef = slab_coef.T
    rows, picked = pl.pallas_call(
        observed_body,
        out_shape=[shape(PER_SLAB, ROWS + BLOCK), shape(BANDS, LONS, PER_BAND)],
        in_specs=[vmem()] * 6,
        out_specs=[vmem()] * 2,
        name="observed",
    )(weights, second_coef, own, north_rows, south_rows, index)

    three, two = pl.pallas_call(
        triple_body,
        out_shape=[shape(18, ROWS + BLOCK), shape(12, ROWS + BLOCK)],
        in_specs=[vmem()] * 3,
        out_specs=[vmem()] * 2,
        name="triple",
    )(rows, along(rows, (0, -1, 0)), along(rows, (0, 1, 0)))
    picked_all = to_all(picked, "band")
    line, block = pl.pallas_call(
        stack_body,
        out_shape=[shape(48, ROWS), shape(BANDS * 8, 48, PER_BAND)],
        in_specs=[vmem()] * 3,
        out_specs=[vmem()] * 2,
        name="stack",
    )(three, along(three, (0, -3, 0)), along(two, (0, 3, 0)))
    blocks = to_all(
        block,
        ("band", "col"),
        [
            [
                b * SLABS + x * 16 + z * 2 + k
                for b in range(BANDS)
                for x in range(4)
                for k in range(2)
            ]
            for z in range(8)
        ],
    )
    east, west = along(line, (-1, 0, 0)), along(line, (1, 0, 0))
    far = [along(east[:24], (-1, 0, 0)), along(west[24:], (1, 0, 0))]
    pieces = [line, east, west] + far
    pieces += [along(piece, (0, 0, 1)) for piece in pieces]

    inverse = pl.pallas_call(
        inverse_first_body,
        out_shape=shape(OBS, OBS),
        in_specs=[vmem()] * 2,
        out_specs=vmem(),
        name="inverse_0",
    )(blocks, noise)
    for step in (1, 2):
        inverse = pl.pallas_call(
            partial(inverse_body, step * BLOCK),
            out_shape=shape(OBS, OBS),
            in_specs=[vmem()],
            out_specs=vmem(),
        )(inverse)

    order = pl.pallas_call(
        order_body,
        out_shape=shape(OBS, OBS),
        out_specs=vmem(),
        name="order",
    )()
    chunk = lambda height: pl.BlockSpec((height, CHUNK), lambda i: (0, i))
    return pl.pallas_call(
        update_body,
        out_shape=shape(LONS, ROWS),
        grid=(4,),
        in_specs=[
            pl.BlockSpec((BANDS, LONS, PER_BAND), lambda i: (0, 0, 0)),
            pl.BlockSpec((OBS, OBS), lambda i: (0, 0)),
            pl.BlockSpec((OBS, OBS), lambda i: (0, 0)),
            pl.BlockSpec((LONS, 8), lambda i: (0, 0)),
        ]
        + [chunk(LONS)] * 3
        + [chunk(h) for h in (48, 48, 48, 24, 24)] * 2,
        out_specs=chunk(LONS),
        scratch_shapes=[pltpu.VMEM((LONS, OBS), F32), pltpu.VMEM((LONS, OBS), F32)],
        name="update",
    )(picked_all, inverse, order, second_coef, advected, north_slab, south_slab, *pieces)


def solution(mesh):
    return jax.shard_map(
        local,
        mesh=mesh,
        in_specs=(P("col", "band"), P(), P(), P(), P(), P()),
        out_specs=P("col", "band"),
        check_vma=False,
    )
```

```python
from functools import partial

import jax
import jax.numpy as jnp
from jax import lax
from jax.experimental import pallas as pl
from jax.experimental.pallas import tpu as pltpu
from jax.sharding import PartitionSpec as P


LATS = 64
LONS = 160
BANDS = 4
SLABS = 64
STRIP = LATS // BANDS
ROWS = STRIP * LONS
BATCHES = 3
PER_SLAB = 6
OBS = SLABS * PER_SLAB
PER_BAND = OBS // BANDS
EDGE = 256
EDGE_START = ROWS - EDGE
EDGE_LOW = EDGE - LONS
HALF = OBS // 2
CHUNK = 640
BLOCK = 128
HIGHEST = lax.Precision.HIGHEST
F32 = jnp.float32


def mm(a, b):
    return lax.dot_general(
        a, b, (((1,), (0,)), ((), ())), precision=HIGHEST, preferred_element_type=F32
    )


def pick(a, chosen):
    chosen = chosen.astype(jnp.bfloat16)
    total = None
    for _ in range(3):
        part = a.astype(jnp.bfloat16)
        a = a - part.astype(F32)
        term = lax.dot_general(
            part, chosen, (((1,), (0,)), ((), ())), preferred_element_type=F32
        )
        total = term if total is None else total + term
    return total


def stencil(east, west, north, south):
    here = (
        1.0
        - jnp.maximum(east, 0.0)
        + jnp.minimum(west, 0.0)
        - jnp.maximum(north, 0.0)
        + jnp.minimum(south, 0.0)
    )
    return [
        here,
        -jnp.minimum(east, 0.0),
        jnp.maximum(west, 0.0),
        -jnp.minimum(north, 0.0),
        jnp.maximum(south, 0.0),
    ]


def westward(wind):
    return jnp.concatenate([wind[:, LONS - 1 :], wind[:, : LONS - 1]], axis=1)


def prepare_body(
    owner, offset, variance, wind_east, wind_north,
    near_out, index_out, noise_out, first_out, second_out, weights_out,
):
    band, col = lax.axis_index("band"), lax.axis_index("col")
    sub = lax.broadcasted_iota(jnp.int32, (BLOCK, BLOCK), 0)
    lane = lax.broadcasted_iota(jnp.int32, (BLOCK, BLOCK), 1)
    target = lax.broadcasted_iota(jnp.int32, (BLOCK, OBS), 1)
    natural = jnp.zeros((1, OBS), jnp.int32)
    offsets = jnp.zeros((1, OBS), jnp.int32)
    noise = jnp.zeros((1, OBS), F32)

    def tall(row):
        return jnp.transpose(jnp.broadcast_to(row, (BLOCK, BLOCK)))

    def wide(v):
        return jnp.concatenate([v] * BATCHES, axis=1)

    for t in range(BATCHES):
        row = owner[t : t + 1, :]
        flat = jnp.broadcast_to(row, (BLOCK, BLOCK))
        same = (flat == jnp.transpose(flat)) & (sub < lane)
        rank = jnp.sum(same.astype(jnp.int32), axis=0, keepdims=True)
        within = 2 * t + rank
        plain = wide(tall(row * PER_SLAB + within)) == target
        lanes = (row // 16) * PER_BAND + (row & 1) * 48 + (row // 2 % 8) * PER_SLAB + within
        hit = wide(tall(lanes)) == target
        away = wide(tall(offset[t : t + 1, :]))
        natural += jnp.sum(jnp.where(plain, away, 0), axis=0, keepdims=True)
        offsets += jnp.sum(jnp.where(hit, away, 0), axis=0, keepdims=True)
        noise += jnp.sum(
            jnp.where(hit, wide(tall(variance[t : t + 1, :])), 0.0), axis=0, keepdims=True
        )
    noise_out[...] = noise
    spread = jnp.broadcast_to(natural, (8, OBS))
    shift = (SLABS + 1 - col) * PER_SLAB
    near = pltpu.roll(spread, lax.rem(shift, OBS), 1)[:, :BLOCK]
    near_out[...] = near
    n = lax.broadcasted_iota(jnp.int32, (8, OBS), 1)
    slab = (n // PER_SLAB % 8) * 2 + n // 48 % 2
    spread = jnp.broadcast_to(offsets, (8, OBS)) + slab * LONS
    points = pltpu.roll(spread, lax.rem(OBS - band * PER_BAND, OBS), 1)[0:1, :BLOCK]
    index_out[...] = jnp.where(lane[0:1, :] < PER_BAND, points, -1)

    start = pl.multiple_of(band * STRIP, STRIP)
    lat = lax.broadcasted_iota(jnp.int32, (STRIP, LONS), 0)
    lon = lax.broadcasted_iota(jnp.int32, (STRIP, LONS), 1)
    east = wind_east[pl.ds(start, STRIP), :]
    north = wind_north[pl.ds(start, STRIP), :]
    before = wind_north[pl.ds(jnp.maximum(band * STRIP - 1, 0), 1), :]
    south = jnp.concatenate([before, north[: STRIP - 1]], axis=0)
    south = jnp.where(lat + start == 0, 0.0, south)
    north = jnp.where(lat + start == LATS - 1, 0.0, north)
    here, to_east, to_west, to_north, to_south = stencil(east, westward(east), north, south)
    kinds = [
        here,
        jnp.where(lon < LONS - 1, to_east, 0.0),
        jnp.where(lon == LONS - 1, to_east, 0.0),
        jnp.where(lon > 0, to_west, 0.0),
        jnp.where(lon == 0, to_west, 0.0),
        jnp.where(lat < STRIP - 1, to_north, 0.0),
        jnp.where(lat > 0, to_south, 0.0),
        jnp.where(lat == 0, to_south, jnp.where(lat == STRIP - 1, to_north, 0.0)),
    ]
    for r in range(STRIP):
        first_out[:, r * LONS : (r + 1) * LONS] = jnp.concatenate(
            [kind[r : r + 1, :] for kind in kinds], axis=0
        )
    flat = first_out[...]
    kind = lax.broadcasted_iota(jnp.int32, (8, ROWS), 0)
    ahead = (kind == 1) | (kind == 2)
    behind = (kind == 3) | (kind == 4)
    first_out[...] = jnp.where(
        ahead, pltpu.roll(flat, 1, 1), jnp.where(behind, pltpu.roll(flat, ROWS - 1, 1), flat)
    )

    east = wind_east[pl.ds(col, 1), :]
    north = wind_north[pl.ds(col, 1), :]
    south = wind_north[pl.ds(jnp.maximum(col - 1, 0), 1), :]
    north = jnp.where(col == LATS - 1, 0.0, north)
    south = jnp.where(col == 0, 0.0, south)
    slab_coef = jnp.concatenate(
        stencil(east, westward(east), north, south) + [jnp.zeros((3, LONS), F32)], axis=0
    )
    second_out[...] = slab_coef
    own = pltpu.roll(near, BLOCK - PER_SLAB, 1)[0:1, :]
    picked = (lax.broadcasted_iota(jnp.int32, (LONS, BLOCK), 0) == own).astype(F32)
    weights = mm(slab_coef, picked)
    weights = jnp.concatenate([weights, jnp.zeros((BLOCK - 8, BLOCK), F32)], axis=0)
    weights_out[...] = jnp.transpose(weights)[:8, :]


def tiles_to_row(v):
    return jnp.concatenate([v[8 * t : 8 * t + 8, :] for t in range(LONS // 8)], axis=1)


def row_to_tiles(v):
    return jnp.concatenate([v[:, BLOCK * t : BLOCK * (t + 1)] for t in range(LONS // 8)], axis=0)


def first_body(
    near_in, weights, c, coef, below, above, index,
    a_out, up_out, down_out, own_out, pair, near, arrived,
):
    fetch = pltpu.make_async_copy(near_in, near, arrived)
    fetch.start()
    for tile in range(LONS // 8):
        rows = slice(8 * tile, 8 * tile + 8)
        q = c[rows, :]
        north, south = pltpu.roll(q, ROWS - LONS, 1), pltpu.roll(q, LONS, 1)
        acc = coef[0:1, :] * q + coef[5:6, :] * north + coef[6:7, :] * south
        acc += pltpu.roll(coef[1:2, :] * q + coef[2:3, :] * south, ROWS - 1, 1)
        acc += pltpu.roll(coef[3:4, :] * q + coef[4:5, :] * north, 1, 1)
        a_out[rows, :] = acc
        a_out[rows, :EDGE] += coef[7:8, :EDGE] * pltpu.roll(below[rows, :], LONS, 1)
        a_out[rows, EDGE_START:] += coef[7:8, EDGE_START:] * pltpu.roll(above[rows, :], EDGE_LOW, 1)
    fetch.wait()
    up_out[:8, :] = jnp.zeros((8, ROWS), F32)
    down_out[:8, :] = jnp.zeros((8, ROWS), F32)
    own_out[:8, :] = jnp.zeros((8, ROWS), F32)
    pair[...] = jnp.zeros(pair.shape, F32)
    for k in range(PER_SLAB):
        up_out[k : k + 1, :] = a_out[pl.ds(near[0, 2 * PER_SLAB + k], 1), :]
        down_out[k : k + 1, :] = a_out[pl.ds(near[0, k], 1), :]
        o = near[0, PER_SLAB + k]
        own_out[k : k + 1, :] = a_out[pl.ds(o, 1), :]
        pair[k : k + 1, :] = a_out[pl.ds(jnp.where(o == LONS - 1, 0, o + 1), 1), :]
        pair[k + 8 : k + 9, :] = a_out[pl.ds(jnp.where(o == 0, LONS - 1, o - 1), 1), :]
    own_out[:8, :] = (
        weights[:, 0:1] * own_out[:8, :]
        + weights[:, 1:2] * pair[:8, :]
        + weights[:, 2:3] * pair[8:, :]
    )
    width = ROWS // 5
    total = jnp.zeros((LONS, BLOCK), F32)
    for part in range(5):
        lanes = lax.broadcasted_iota(jnp.int32, (width, BLOCK), 0) + part * width
        total += pick(a_out[:, part * width : (part + 1) * width], lanes == index[...])
    packed = tiles_to_row(total)
    for ref in (up_out, down_out, own_out):
        ref[8:, :] = packed


def observed_body(weights, coef, own, north, south, index, rows_out, picked_out):
    rows = own[:8, :] + weights[:, 3:4] * north[:8, :] + weights[:, 4:5] * south[:8, :]
    rows_out[:, :ROWS] = rows[:PER_SLAB, :]
    width = ROWS // 5
    total = jnp.zeros((8, BLOCK), F32)
    for part in range(5):
        lanes = lax.broadcasted_iota(jnp.int32, (width, BLOCK), 0) + part * width
        total += pick(rows[:, part * width : (part + 1) * width], lanes == index[...])
    rows_out[:, ROWS:] = total[:PER_SLAB, :]
    q = row_to_tiles(own[8:, :])
    picked = second_step(coef, q, row_to_tiles(north[8:, :]), row_to_tiles(south[8:, :]))
    for band in range(BANDS):
        picked_out[band] = picked[:, :PER_BAND]


def second_step(coef, q, north, south):
    return (
        coef[:, 0:1] * q
        + coef[:, 1:2] * pltpu.roll(q, LONS - 1, 0)
        + coef[:, 2:3] * pltpu.roll(q, 1, 0)
        + coef[:, 3:4] * north
        + coef[:, 4:5] * south
    )


def inverse_2(a, b, d):
    scale = 1.0 / (a * d - b * b)
    return d * scale, -b * scale, a * scale


def dots(left, right):
    terms = [l * r for l, r in zip(left, right)]
    while len(terms) > 1:
        odd = terms[len(terms) // 2 * 2 :]
        terms = [u + v for u, v in zip(terms[::2], terms[1::2])] + odd
    return terms[0]


def inverse_4(p):
    a00, a01, a11 = inverse_2(p[0][0], p[0][1], p[1][1])
    y00 = a00 * p[0][2] + a01 * p[1][2]
    y01 = a00 * p[0][3] + a01 * p[1][3]
    y10 = a01 * p[0][2] + a11 * p[1][2]
    y11 = a01 * p[0][3] + a11 * p[1][3]
    s00 = p[2][2] - (p[0][2] * y00 + p[1][2] * y10)
    s01 = p[2][3] - (p[0][2] * y01 + p[1][2] * y11)
    s11 = p[3][3] - (p[0][3] * y01 + p[1][3] * y11)
    d00, d01, d11 = inverse_2(s00, s01, s11)
    z00 = y00 * d00 + y01 * d01
    z01 = y00 * d01 + y01 * d11
    z10 = y10 * d00 + y11 * d01
    z11 = y10 * d01 + y11 * d11
    b00 = a00 + (z00 * y00 + z01 * y01)
    b01 = a01 + (z00 * y10 + z01 * y11)
    b11 = a11 + (z10 * y10 + z11 * y11)
    return [
        [b00, b01, -z00, -z01],
        [b01, b11, -z10, -z11],
        [-z00, -z10, d00, d01],
        [-z01, -z11, d01, d11],
    ]


def inverse_block(m):
    n = BLOCK
    lane = lax.broadcasted_iota(jnp.int32, (8, n), 1)
    sub = lax.broadcasted_iota(jnp.int32, (8, n), 0)
    tiles = [m[8 * t : 8 * t + 8, :] for t in range(n // 8)]
    half = range(4)
    for home in range(n // 8):
        j = 8 * home
        inside = (lane >= j) & (lane < j + 8)
        order = [home] + [t for t in range(n // 8) if t != home]
        order = order[:1] + [t for t in order if t == home + 1] + [t for t in order[1:] if t != home + 1]
        columns = {}
        for t in order:
            columns[t] = [
                jnp.take_along_axis(tiles[t], jnp.full((8, n), j + k, jnp.int32), axis=1)
                for k in range(8)
            ]
        p = [
            [
                jnp.broadcast_to(columns[home][max(i, k)][min(i, k) : min(i, k) + 1, :], (8, n))
                for k in range(8)
            ]
            for i in range(8)
        ]
        p12 = [p[i][4:] for i in half]
        first = inverse_4([p[i][:4] for i in half])
        y = [[dots(first[i], [p12[k][q] for k in half]) for q in half] for i in half]
        schur = [[None] * 4 for _ in half]
        for i in half:
            for q in range(i, 4):
                schur[i][q] = p[4 + i][4 + q] - dots(
                    [p12[k][i] for k in half], [y[k][q] for k in half]
                )
                schur[q][i] = schur[i][q]
        second = inverse_4(schur)
        rows = [
            jnp.where(
                inside,
                jnp.where(lane == j + i, 1.0, 0.0),
                jnp.broadcast_to(tiles[home][i : i + 1, :], (8, n)),
            )
            for i in range(8)
        ]
        top = [dots(first[i], rows[:4]) for i in half]
        low = [rows[4 + i] - dots([p12[k][i] for k in half], top) for i in half]
        low = [dots(second[i], low) for i in half]
        top = [top[i] - dots(y[i], low) for i in half]
        t = top + low
        swept = []
        for number, tile in enumerate(tiles):
            if number == home:
                new = t[0]
                for i in range(1, 8):
                    new = jnp.where(sub == i, t[i], new)
            else:
                new = jnp.where(inside, 0.0, tile) - dots(columns[number], t)
            swept.append(new)
        tiles = swept
    return jnp.concatenate(tiles, axis=0)


def sweep(out, at):
    inv = inverse_block(out[at : at + BLOCK, at : at + BLOCK])
    row_id = lax.broadcasted_iota(jnp.int32, (OBS, BLOCK), 0)
    column = out[:, at : at + BLOCK]
    column = jnp.where((row_id >= at) & (row_id < at + BLOCK), 0.0, column)
    out[:, at : at + BLOCK] = jnp.zeros((OBS, BLOCK), F32)
    top = mm(inv, out[at : at + BLOCK, :])
    lane = lax.broadcasted_iota(jnp.int32, (BLOCK, OBS), 1)
    inv_wide = jnp.concatenate([inv] * (OBS // BLOCK), axis=1)
    top = jnp.where((lane >= at) & (lane < at + BLOCK), inv_wide, top)
    out[at : at + BLOCK, :] = top
    out[...] -= mm(column, top)


def inverse_first_body(blocks, noise, out):
    for b in range(BANDS):
        for part in range(8):
            out[part * 48 : part * 48 + 48, b * PER_BAND : (b + 1) * PER_BAND] = blocks[
                b * 8 + part
            ]
    r = lax.broadcasted_iota(jnp.int32, (OBS, OBS), 0)
    c = lax.broadcasted_iota(jnp.int32, (OBS, OBS), 1)
    out[...] += jnp.where(r == c, noise[...], 0.0)
    sweep(out, 0)


def inverse_body(at, before, out):
    out[...] = before[...]
    sweep(out, at)


def triple_body(own, above, below, three_out, two_out):
    rows = jnp.concatenate([own[...], above[...], below[...]], axis=0)
    three_out[...] = rows
    two_out[...] = rows[:12, :]


Z_AWAY = (0, 1, -1, 3, 4, 2, -3, -2)
X_AWAY = (0, 1, -1, 2)


def away(j, steps):
    return sum(jnp.where(j == i, step, 0) for i, step in enumerate(steps))


def stack_body(near, above, below, line_out, block_out):
    rows = jnp.concatenate([near[...], above[...], below[...]], axis=0)
    line_out[...] = rows[:, :ROWS]
    n = lax.broadcasted_iota(jnp.int32, (48, 48), 1)
    r = lax.broadcasted_iota(jnp.int32, (48, 48), 0)
    z = (lax.axis_index("col") // 2 + away(n // PER_SLAB, Z_AWAY)) & 7
    sort = (r == z * PER_SLAB + n % PER_SLAB).astype(F32)
    block = mm(sort, rows[:, ROWS:])[:, :PER_BAND]
    for copy in range(BANDS * 8):
        block_out[copy] = block


def order_body(out):
    col = lax.axis_index("col")
    r = lax.broadcasted_iota(jnp.int32, (OBS, OBS), 0)
    n = lax.broadcasted_iota(jnp.int32, (1, OBS), 1)
    core = (n // HALF + col) & 1
    x = (col // 16 + (1 - 2 * core) * away(n // 48 % 4, X_AWAY)) & 3
    z = (col // 2 + away(n // PER_SLAB % 8, Z_AWAY)) & 7
    out[...] = (r == x * PER_BAND + core * 48 + z * PER_SLAB + n % PER_SLAB).astype(F32)


def parts(v):
    high = v.astype(jnp.bfloat16)
    return high, (v - high.astype(F32)).astype(jnp.bfloat16)


def mm_3(a, b):
    a_high, a_low = parts(a)
    b_high, b_low = parts(b)
    dot = lambda u, v: lax.dot_general(
        u, v, (((1,), (0,)), ((), ())), preferred_element_type=F32
    )
    return dot(a_high, b_high) + (dot(a_high, b_low) + dot(a_low, b_high))


def update_body(picked, inverse, order, coef, a, north, south, *refs):
    pieces, (out, gain, wide) = refs[:-3], refs[-3:]

    @pl.when(pl.program_id(0) == 0)
    def _():
        for b in range(BANDS):
            wide[:, b * PER_BAND : (b + 1) * PER_BAND] = picked[b]
        gain[...] = mm(mm(wide[...], inverse[...]), order[...])

    rows = jnp.concatenate([piece[...] for piece in pieces], axis=0)
    out[...] = second_step(coef, a[...], north[...], south[...]) - mm_3(gain[...], rows)


def vmem():
    return pl.BlockSpec(memory_space=pltpu.VMEM)


def shape(*dims):
    return jax.ShapeDtypeStruct(dims, F32)


def split_col(c):
    return c // 16, (c // 2) % 8, c % 2


def move(c, step):
    x, z, k = (a + b for a, b in zip(split_col(c), step))
    return x % 4 * 16 + z % 8 * 2 + k % 2


def to_all(copies, axis, groups=None):
    return lax.all_to_all(copies, axis, 0, 0, tiled=True, axis_index_groups=groups)


def local(covariance, wind_east, wind_north, obs_owner, obs_offset, obs_variance):
    up_band = [(i, i + 1) for i in range(BANDS - 1)]
    down_band = [(i + 1, i) for i in range(BANDS - 1)]
    up_col = [(i, i + 1) for i in range(SLABS - 1)]
    down_col = [(i + 1, i) for i in range(SLABS - 1)]

    def along(value, step):
        pairs = [(c, move(c, step)) for c in range(SLABS)]
        return lax.ppermute(value, "col", pairs)

    def beside(value, step):
        pairs = [(c, move(c, (step * (2 * (c % 2) - 1), 0, 0))) for c in range(SLABS)]
        return lax.ppermute(value, "col", pairs)

    below = lax.ppermute(covariance[:, EDGE_START:], "band", up_band)
    above = lax.ppermute(covariance[:, :EDGE], "band", down_band)

    near, index, noise, first_coef, slab_coef, weights = pl.pallas_call(
        prepare_body,
        out_shape=[
            jax.ShapeDtypeStruct((8, BLOCK), jnp.int32),
            jax.ShapeDtypeStruct((1, BLOCK), jnp.int32),
            shape(1, OBS),
            shape(8, ROWS),
            shape(8, LONS),
            shape(8, BLOCK),
        ],
        in_specs=[vmem()] * 5,
        out_specs=[vmem()] * 6,
        name="prepare",
    )(obs_owner, obs_offset, obs_variance, wind_east, wind_north)

    advected, for_up, for_down, own = pl.pallas_call(
        first_body,
        out_shape=[shape(LONS, ROWS)] + [shape(16, ROWS)] * 3,
        in_specs=[vmem()] * 7,
        out_specs=[vmem()] * 4,
        scratch_shapes=[
            pltpu.VMEM((16, ROWS), F32),
            pltpu.SMEM((8, BLOCK), jnp.int32),
            pltpu.SemaphoreType.DMA,
        ],
        name="first",
    )(near, weights, covariance, first_coef, below, above, index)

    south_rows = lax.ppermute(for_up, "col", up_col)
    north_rows = lax.ppermute(for_down, "col", down_col)
    south_slab = lax.ppermute(advected, "col", up_col)
    north_slab = lax.ppermute(advected, "col", down_col)

    second_coef = slab_coef.T
    rows, picked = pl.pallas_call(
        observed_body,
        out_shape=[shape(PER_SLAB, ROWS + BLOCK), shape(BANDS, LONS, PER_BAND)],
        in_specs=[vmem()] * 6,
        out_specs=[vmem()] * 2,
        name="observed",
    )(weights, second_coef, own, north_rows, south_rows, index)

    three, two = pl.pallas_call(
        triple_body,
        out_shape=[shape(18, ROWS + BLOCK), shape(12, ROWS + BLOCK)],
        in_specs=[vmem()] * 3,
        out_specs=[vmem()] * 2,
        name="triple",
    )(rows, along(rows, (0, -1, 0)), along(rows, (0, 1, 0)))
    picked_all = to_all(picked, "band")
    line, block = pl.pallas_call(
        stack_body,
        out_shape=[shape(48, ROWS), shape(BANDS * 8, 48, PER_BAND)],
        in_specs=[vmem()] * 3,
        out_specs=[vmem()] * 2,
        name="stack",
    )(three, along(three, (0, -3, 0)), along(two, (0, 3, 0)))
    blocks = to_all(
        block,
        ("band", "col"),
        [
            [
                b * SLABS + x * 16 + z * 2 + k
                for b in range(BANDS)
                for x in range(4)
                for k in range(2)
            ]
            for z in range(8)
        ],
    )
    pieces = [line, beside(line, 1), beside(line, -1)]
    pieces.append(beside(pieces[1], 1))
    pieces += [along(piece, (0, 0, 1)) for piece in pieces]

    inverse = pl.pallas_call(
        inverse_first_body,
        out_shape=shape(OBS, OBS),
        in_specs=[vmem()] * 2,
        out_specs=vmem(),
        name="inverse_0",
    )(blocks, noise)
    for step in (1, 2):
        inverse = pl.pallas_call(
            partial(inverse_body, step * BLOCK),
            out_shape=shape(OBS, OBS),
            in_specs=[vmem()],
            out_specs=vmem(),
        )(inverse)

    order = pl.pallas_call(
        order_body,
        out_shape=shape(OBS, OBS),
        out_specs=vmem(),
        name="order",
    )()
    chunk = lambda height: pl.BlockSpec((height, CHUNK), lambda i: (0, i))
    return pl.pallas_call(
        update_body,
        out_shape=shape(LONS, ROWS),
        grid=(ROWS // CHUNK,),
        in_specs=[
            pl.BlockSpec((BANDS, LONS, PER_BAND), lambda i: (0, 0, 0)),
            pl.BlockSpec((OBS, OBS), lambda i: (0, 0)),
            pl.BlockSpec((OBS, OBS), lambda i: (0, 0)),
            pl.BlockSpec((LONS, 8), lambda i: (0, 0)),
        ]
        + [chunk(LONS)] * 3
        + [chunk(48)] * 8,
        out_specs=chunk(LONS),
        scratch_shapes=[pltpu.VMEM((LONS, OBS), F32), pltpu.VMEM((LONS, OBS), F32)],
        name="update",
    )(picked_all, inverse, order, second_coef, advected, north_slab, south_slab, *pieces)


def solution(mesh):
    return jax.shard_map(
        local,
        mesh=mesh,
        in_specs=(P("col", "band"), P(), P(), P(), P(), P()),
        out_specs=P("col", "band"),
        check_vma=False,
    )
```

```python
from functools import partial

import jax
import jax.numpy as jnp
from jax import lax
from jax.experimental import pallas as pl
from jax.experimental.pallas import tpu as pltpu
from jax.sharding import PartitionSpec as P


LATS = 64
LONS = 160
BANDS = 4
SLABS = 64
STRIP = LATS // BANDS
ROWS = STRIP * LONS
BATCHES = 3
PER_SLAB = 6
OBS = SLABS * PER_SLAB
PER_BAND = OBS // BANDS
EDGE = 256
EDGE_START = ROWS - EDGE
EDGE_LOW = EDGE - LONS
HALF = OBS // 2
CHUNK = 640
BLOCK = 128
HIGHEST = lax.Precision.HIGHEST
F32 = jnp.float32


def mm(a, b):
    return lax.dot_general(
        a, b, (((1,), (0,)), ((), ())), precision=HIGHEST, preferred_element_type=F32
    )


def pick(a, chosen):
    chosen = chosen.astype(jnp.bfloat16)
    total = None
    for _ in range(3):
        part = a.astype(jnp.bfloat16)
        a = a - part.astype(F32)
        term = lax.dot_general(
            part, chosen, (((1,), (0,)), ((), ())), preferred_element_type=F32
        )
        total = term if total is None else total + term
    return total


def stencil(east, west, north, south):
    here = (
        1.0
        - jnp.maximum(east, 0.0)
        + jnp.minimum(west, 0.0)
        - jnp.maximum(north, 0.0)
        + jnp.minimum(south, 0.0)
    )
    return [
        here,
        -jnp.minimum(east, 0.0),
        jnp.maximum(west, 0.0),
        -jnp.minimum(north, 0.0),
        jnp.maximum(south, 0.0),
    ]


def westward(wind):
    return jnp.concatenate([wind[:, LONS - 1 :], wind[:, : LONS - 1]], axis=1)


def prepare_body(
    owner, offset, variance, wind_east, wind_north,
    near_out, index_out, noise_out, first_out, second_out, weights_out,
):
    band, col = lax.axis_index("band"), lax.axis_index("col")
    sub = lax.broadcasted_iota(jnp.int32, (BLOCK, BLOCK), 0)
    lane = lax.broadcasted_iota(jnp.int32, (BLOCK, BLOCK), 1)
    target = lax.broadcasted_iota(jnp.int32, (BLOCK, OBS), 1)
    natural = jnp.zeros((1, OBS), jnp.int32)
    offsets = jnp.zeros((1, OBS), jnp.int32)
    noise = jnp.zeros((1, OBS), F32)

    def tall(row):
        return jnp.transpose(jnp.broadcast_to(row, (BLOCK, BLOCK)))

    def wide(v):
        return jnp.concatenate([v] * BATCHES, axis=1)

    for t in range(BATCHES):
        row = owner[t : t + 1, :]
        flat = jnp.broadcast_to(row, (BLOCK, BLOCK))
        same = (flat == jnp.transpose(flat)) & (sub < lane)
        rank = jnp.sum(same.astype(jnp.int32), axis=0, keepdims=True)
        within = 2 * t + rank
        plain = wide(tall(row * PER_SLAB + within)) == target
        lanes = (row // 16) * PER_BAND + (row & 1) * 48 + (row // 2 % 8) * PER_SLAB + within
        hit = wide(tall(lanes)) == target
        away = wide(tall(offset[t : t + 1, :]))
        natural += jnp.sum(jnp.where(plain, away, 0), axis=0, keepdims=True)
        offsets += jnp.sum(jnp.where(hit, away, 0), axis=0, keepdims=True)
        noise += jnp.sum(
            jnp.where(hit, wide(tall(variance[t : t + 1, :])), 0.0), axis=0, keepdims=True
        )
    noise_out[...] = noise
    spread = jnp.broadcast_to(natural, (8, OBS))
    shift = (SLABS + 1 - col) * PER_SLAB
    near = pltpu.roll(spread, lax.rem(shift, OBS), 1)[:, :BLOCK]
    near_out[...] = near
    n = lax.broadcasted_iota(jnp.int32, (8, OBS), 1)
    slab = (n // PER_SLAB % 8) * 2 + n // 48 % 2
    spread = jnp.broadcast_to(offsets, (8, OBS)) + slab * LONS
    points = pltpu.roll(spread, lax.rem(OBS - band * PER_BAND, OBS), 1)[0:1, :BLOCK]
    index_out[...] = jnp.where(lane[0:1, :] < PER_BAND, points, -1)

    start = pl.multiple_of(band * STRIP, STRIP)
    lat = lax.broadcasted_iota(jnp.int32, (STRIP, LONS), 0)
    lon = lax.broadcasted_iota(jnp.int32, (STRIP, LONS), 1)
    east = wind_east[pl.ds(start, STRIP), :]
    north = wind_north[pl.ds(start, STRIP), :]
    before = wind_north[pl.ds(jnp.maximum(band * STRIP - 1, 0), 1), :]
    south = jnp.concatenate([before, north[: STRIP - 1]], axis=0)
    south = jnp.where(lat + start == 0, 0.0, south)
    north = jnp.where(lat + start == LATS - 1, 0.0, north)
    here, to_east, to_west, to_north, to_south = stencil(east, westward(east), north, south)
    kinds = [
        here,
        jnp.where(lon < LONS - 1, to_east, 0.0),
        jnp.where(lon == LONS - 1, to_east, 0.0),
        jnp.where(lon > 0, to_west, 0.0),
        jnp.where(lon == 0, to_west, 0.0),
        jnp.where(lat < STRIP - 1, to_north, 0.0),
        jnp.where(lat > 0, to_south, 0.0),
        jnp.where(lat == 0, to_south, jnp.where(lat == STRIP - 1, to_north, 0.0)),
    ]
    for r in range(STRIP):
        first_out[:, r * LONS : (r + 1) * LONS] = jnp.concatenate(
            [kind[r : r + 1, :] for kind in kinds], axis=0
        )
    flat = first_out[...]
    kind = lax.broadcasted_iota(jnp.int32, (8, ROWS), 0)
    ahead = (kind == 1) | (kind == 2)
    behind = (kind == 3) | (kind == 4)
    first_out[...] = jnp.where(
        ahead, pltpu.roll(flat, 1, 1), jnp.where(behind, pltpu.roll(flat, ROWS - 1, 1), flat)
    )

    east = wind_east[pl.ds(col, 1), :]
    north = wind_north[pl.ds(col, 1), :]
    south = wind_north[pl.ds(jnp.maximum(col - 1, 0), 1), :]
    north = jnp.where(col == LATS - 1, 0.0, north)
    south = jnp.where(col == 0, 0.0, south)
    slab_coef = jnp.concatenate(
        stencil(east, westward(east), north, south) + [jnp.zeros((3, LONS), F32)], axis=0
    )
    second_out[...] = slab_coef
    own = pltpu.roll(near, BLOCK - PER_SLAB, 1)[0:1, :]
    picked = (lax.broadcasted_iota(jnp.int32, (LONS, BLOCK), 0) == own).astype(F32)
    weights = mm(slab_coef, picked)
    weights = jnp.concatenate([weights, jnp.zeros((BLOCK - 8, BLOCK), F32)], axis=0)
    weights_out[...] = jnp.transpose(weights)[:8, :]


def tiles_to_row(v):
    return jnp.concatenate([v[8 * t : 8 * t + 8, :] for t in range(LONS // 8)], axis=1)


def row_to_tiles(v):
    return jnp.concatenate([v[:, BLOCK * t : BLOCK * (t + 1)] for t in range(LONS // 8)], axis=0)


def first_body(
    near_in, weights, c, coef, below, above, index,
    a_out, up_out, down_out, own_out, pair, near, arrived,
):
    fetch = pltpu.make_async_copy(near_in, near, arrived)
    fetch.start()
    for tile in range(LONS // 8):
        rows = slice(8 * tile, 8 * tile + 8)
        q = c[rows, :]
        north, south = pltpu.roll(q, ROWS - LONS, 1), pltpu.roll(q, LONS, 1)
        acc = coef[0:1, :] * q + coef[5:6, :] * north + coef[6:7, :] * south
        acc += pltpu.roll(coef[1:2, :] * q + coef[2:3, :] * south, ROWS - 1, 1)
        acc += pltpu.roll(coef[3:4, :] * q + coef[4:5, :] * north, 1, 1)
        a_out[rows, :] = acc
        a_out[rows, :EDGE] += coef[7:8, :EDGE] * pltpu.roll(below[rows, :], LONS, 1)
        a_out[rows, EDGE_START:] += coef[7:8, EDGE_START:] * pltpu.roll(above[rows, :], EDGE_LOW, 1)
    fetch.wait()
    up_out[:8, :] = jnp.zeros((8, ROWS), F32)
    down_out[:8, :] = jnp.zeros((8, ROWS), F32)
    own_out[:8, :] = jnp.zeros((8, ROWS), F32)
    pair[...] = jnp.zeros(pair.shape, F32)
    for k in range(PER_SLAB):
        up_out[k : k + 1, :] = a_out[pl.ds(near[0, 2 * PER_SLAB + k], 1), :]
        down_out[k : k + 1, :] = a_out[pl.ds(near[0, k], 1), :]
        o = near[0, PER_SLAB + k]
        own_out[k : k + 1, :] = a_out[pl.ds(o, 1), :]
        pair[k : k + 1, :] = a_out[pl.ds(jnp.where(o == LONS - 1, 0, o + 1), 1), :]
        pair[k + 8 : k + 9, :] = a_out[pl.ds(jnp.where(o == 0, LONS - 1, o - 1), 1), :]
    own_out[:8, :] = (
        weights[:, 0:1] * own_out[:8, :]
        + weights[:, 1:2] * pair[:8, :]
        + weights[:, 2:3] * pair[8:, :]
    )
    width = ROWS // 5
    total = jnp.zeros((LONS, BLOCK), F32)
    for part in range(5):
        lanes = lax.broadcasted_iota(jnp.int32, (width, BLOCK), 0) + part * width
        total += pick(a_out[:, part * width : (part + 1) * width], lanes == index[...])
    packed = tiles_to_row(total)
    for ref in (up_out, down_out, own_out):
        ref[8:, :] = packed


def observed_body(weights, coef, own, north, south, index, rows_out, picked_out):
    rows = own[:8, :] + weights[:, 3:4] * north[:8, :] + weights[:, 4:5] * south[:8, :]
    rows_out[:, :ROWS] = rows[:PER_SLAB, :]
    width = ROWS // 5
    total = jnp.zeros((8, BLOCK), F32)
    for part in range(5):
        lanes = lax.broadcasted_iota(jnp.int32, (width, BLOCK), 0) + part * width
        total += pick(rows[:, part * width : (part + 1) * width], lanes == index[...])
    rows_out[:, ROWS:] = total[:PER_SLAB, :]
    q = row_to_tiles(own[8:, :])
    picked = second_step(coef, q, row_to_tiles(north[8:, :]), row_to_tiles(south[8:, :]))
    for band in range(BANDS):
        picked_out[band] = picked[:, :PER_BAND]


def second_step(coef, q, north, south):
    return (
        coef[:, 0:1] * q
        + coef[:, 1:2] * pltpu.roll(q, LONS - 1, 0)
        + coef[:, 2:3] * pltpu.roll(q, 1, 0)
        + coef[:, 3:4] * north
        + coef[:, 4:5] * south
    )


def inverse_2(a, b, d):
    scale = 1.0 / (a * d - b * b)
    return d * scale, -b * scale, a * scale


def dots(left, right):
    terms = [l * r for l, r in zip(left, right)]
    while len(terms) > 1:
        odd = terms[len(terms) // 2 * 2 :]
        terms = [u + v for u, v in zip(terms[::2], terms[1::2])] + odd
    return terms[0]


def inverse_4(p):
    a00, a01, a11 = inverse_2(p[0][0], p[0][1], p[1][1])
    y00 = a00 * p[0][2] + a01 * p[1][2]
    y01 = a00 * p[0][3] + a01 * p[1][3]
    y10 = a01 * p[0][2] + a11 * p[1][2]
    y11 = a01 * p[0][3] + a11 * p[1][3]
    s00 = p[2][2] - (p[0][2] * y00 + p[1][2] * y10)
    s01 = p[2][3] - (p[0][2] * y01 + p[1][2] * y11)
    s11 = p[3][3] - (p[0][3] * y01 + p[1][3] * y11)
    d00, d01, d11 = inverse_2(s00, s01, s11)
    z00 = y00 * d00 + y01 * d01
    z01 = y00 * d01 + y01 * d11
    z10 = y10 * d00 + y11 * d01
    z11 = y10 * d01 + y11 * d11
    b00 = a00 + (z00 * y00 + z01 * y01)
    b01 = a01 + (z00 * y10 + z01 * y11)
    b11 = a11 + (z10 * y10 + z11 * y11)
    return [
        [b00, b01, -z00, -z01],
        [b01, b11, -z10, -z11],
        [-z00, -z10, d00, d01],
        [-z01, -z11, d01, d11],
    ]


def inverse_block(m):
    n = BLOCK
    lane = lax.broadcasted_iota(jnp.int32, (8, n), 1)
    sub = lax.broadcasted_iota(jnp.int32, (8, n), 0)
    tiles = [m[8 * t : 8 * t + 8, :] for t in range(n // 8)]
    half = range(4)
    for home in range(n // 8):
        j = 8 * home
        inside = (lane >= j) & (lane < j + 8)
        order = [home] + [t for t in range(n // 8) if t != home]
        order = order[:1] + [t for t in order if t == home + 1] + [t for t in order[1:] if t != home + 1]
        columns = {}
        for t in order:
            columns[t] = [
                jnp.take_along_axis(tiles[t], jnp.full((8, n), j + k, jnp.int32), axis=1)
                for k in range(8)
            ]
        p = [
            [
                jnp.broadcast_to(columns[home][max(i, k)][min(i, k) : min(i, k) + 1, :], (8, n))
                for k in range(8)
            ]
            for i in range(8)
        ]
        p12 = [p[i][4:] for i in half]
        first = inverse_4([p[i][:4] for i in half])
        y = [[dots(first[i], [p12[k][q] for k in half]) for q in half] for i in half]
        schur = [[None] * 4 for _ in half]
        for i in half:
            for q in range(i, 4):
                schur[i][q] = p[4 + i][4 + q] - dots(
                    [p12[k][i] for k in half], [y[k][q] for k in half]
                )
                schur[q][i] = schur[i][q]
        second = inverse_4(schur)
        rows = [
            jnp.where(
                inside,
                jnp.where(lane == j + i, 1.0, 0.0),
                jnp.broadcast_to(tiles[home][i : i + 1, :], (8, n)),
            )
            for i in range(8)
        ]
        top = [dots(first[i], rows[:4]) for i in half]
        low = [rows[4 + i] - dots([p12[k][i] for k in half], top) for i in half]
        low = [dots(second[i], low) for i in half]
        top = [top[i] - dots(y[i], low) for i in half]
        t = top + low
        swept = []
        for number, tile in enumerate(tiles):
            if number == home:
                new = t[0]
                for i in range(1, 8):
                    new = jnp.where(sub == i, t[i], new)
            else:
                new = jnp.where(inside, 0.0, tile) - dots(columns[number], t)
            swept.append(new)
        tiles = swept
    return jnp.concatenate(tiles, axis=0)


def sweep(out, at):
    inv = inverse_block(out[at : at + BLOCK, at : at + BLOCK])
    row_id = lax.broadcasted_iota(jnp.int32, (OBS, BLOCK), 0)
    column = out[:, at : at + BLOCK]
    column = jnp.where((row_id >= at) & (row_id < at + BLOCK), 0.0, column)
    out[:, at : at + BLOCK] = jnp.zeros((OBS, BLOCK), F32)
    top = mm(inv, out[at : at + BLOCK, :])
    lane = lax.broadcasted_iota(jnp.int32, (BLOCK, OBS), 1)
    inv_wide = jnp.concatenate([inv] * (OBS // BLOCK), axis=1)
    top = jnp.where((lane >= at) & (lane < at + BLOCK), inv_wide, top)
    out[at : at + BLOCK, :] = top
    out[...] -= mm(column, top)


def inverse_first_body(blocks, noise, out):
    for b in range(BANDS):
        for part in range(8):
            out[part * 48 : part * 48 + 48, b * PER_BAND : (b + 1) * PER_BAND] = blocks[
                b * 8 + part
            ]
    r = lax.broadcasted_iota(jnp.int32, (OBS, OBS), 0)
    c = lax.broadcasted_iota(jnp.int32, (OBS, OBS), 1)
    out[...] += jnp.where(r == c, noise[...], 0.0)
    sweep(out, 0)


def inverse_body(at, before, out):
    out[...] = before[...]
    sweep(out, at)


def triple_body(own, above, below, three_out, two_out, three_blocks_out, two_blocks_out):
    rows = jnp.concatenate([own[...], above[...], below[...]], axis=0)
    three_out[...] = rows[:, :ROWS]
    two_out[...] = rows[:12, :ROWS]
    three_blocks_out[...] = rows[:, ROWS:]
    two_blocks_out[...] = rows[:12, ROWS:]


Z_AWAY = (0, 1, -1, 3, 4, 2, -3, -2)
X_AWAY = (0, 1, -1, 2)


def away(j, steps):
    return sum(jnp.where(j == i, step, 0) for i, step in enumerate(steps))


def sort_body(near, above, below, block_out):
    rows = jnp.concatenate([near[...], above[...], below[...]], axis=0)
    n = lax.broadcasted_iota(jnp.int32, (48, 48), 1)
    r = lax.broadcasted_iota(jnp.int32, (48, 48), 0)
    z = (lax.axis_index("col") // 2 + away(n // PER_SLAB, Z_AWAY)) & 7
    sort = (r == z * PER_SLAB + n % PER_SLAB).astype(F32)
    block = mm(sort, rows)[:, :PER_BAND]
    for copy in range(BANDS * 8):
        block_out[copy] = block


def stack_body(near, above, below, line_out):
    line_out[...] = jnp.concatenate([near[...], above[...], below[...]], axis=0)


def order_body(out):
    col = lax.axis_index("col")
    r = lax.broadcasted_iota(jnp.int32, (OBS, OBS), 0)
    n = lax.broadcasted_iota(jnp.int32, (1, OBS), 1)
    core = (n // HALF + col) & 1
    x = (col // 16 + (1 - 2 * core) * away(n // 48 % 4, X_AWAY)) & 3
    z = (col // 2 + away(n // PER_SLAB % 8, Z_AWAY)) & 7
    out[...] = (r == x * PER_BAND + core * 48 + z * PER_SLAB + n % PER_SLAB).astype(F32)


def parts(v):
    high = v.astype(jnp.bfloat16)
    return high, (v - high.astype(F32)).astype(jnp.bfloat16)


def mm_3(a, b):
    a_high, a_low = parts(a)
    b_high, b_low = parts(b)
    dot = lambda u, v: lax.dot_general(
        u, v, (((1,), (0,)), ((), ())), preferred_element_type=F32
    )
    return dot(a_high, b_high) + (dot(a_high, b_low) + dot(a_low, b_high))


def update_body(picked, inverse, order, coef, a, north, south, *refs):
    pieces, (out, gain, wide) = refs[:-3], refs[-3:]

    @pl.when(pl.program_id(0) == 0)
    def _():
        for b in range(BANDS):
            wide[:, b * PER_BAND : (b + 1) * PER_BAND] = picked[b]
        gain[...] = pick(mm(wide[...], inverse[...]), order[...])

    rows = jnp.concatenate([piece[...] for piece in pieces], axis=0)
    out[...] = second_step(coef, a[...], north[...], south[...]) - mm_3(gain[...], rows)


def vmem():
    return pl.BlockSpec(memory_space=pltpu.VMEM)


def shape(*dims):
    return jax.ShapeDtypeStruct(dims, F32)


def split_col(c):
    return c // 16, (c // 2) % 8, c % 2


def move(c, step):
    x, z, k = (a + b for a, b in zip(split_col(c), step))
    return x % 4 * 16 + z % 8 * 2 + k % 2


def to_all(copies, axis, groups=None):
    return lax.all_to_all(copies, axis, 0, 0, tiled=True, axis_index_groups=groups)


def local(covariance, wind_east, wind_north, obs_owner, obs_offset, obs_variance):
    up_band = [(i, i + 1) for i in range(BANDS - 1)]
    down_band = [(i + 1, i) for i in range(BANDS - 1)]
    up_col = [(i, i + 1) for i in range(SLABS - 1)]
    down_col = [(i + 1, i) for i in range(SLABS - 1)]

    def along(value, step):
        pairs = [(c, move(c, step)) for c in range(SLABS)]
        return lax.ppermute(value, "col", pairs)

    def beside(value, step):
        pairs = [(c, move(c, (step * (2 * (c % 2) - 1), 0, 0))) for c in range(SLABS)]
        return lax.ppermute(value, "col", pairs)

    below = lax.ppermute(covariance[:, EDGE_START:], "band", up_band)
    above = lax.ppermute(covariance[:, :EDGE], "band", down_band)

    near, index, noise, first_coef, slab_coef, weights = pl.pallas_call(
        prepare_body,
        out_shape=[
            jax.ShapeDtypeStruct((8, BLOCK), jnp.int32),
            jax.ShapeDtypeStruct((1, BLOCK), jnp.int32),
            shape(1, OBS),
            shape(8, ROWS),
            shape(8, LONS),
            shape(8, BLOCK),
        ],
        in_specs=[vmem()] * 5,
        out_specs=[vmem()] * 6,
        name="prepare",
    )(obs_owner, obs_offset, obs_variance, wind_east, wind_north)

    advected, for_up, for_down, own = pl.pallas_call(
        first_body,
        out_shape=[shape(LONS, ROWS)] + [shape(16, ROWS)] * 3,
        in_specs=[vmem()] * 7,
        out_specs=[vmem()] * 4,
        scratch_shapes=[
            pltpu.VMEM((16, ROWS), F32),
            pltpu.SMEM((8, BLOCK), jnp.int32),
            pltpu.SemaphoreType.DMA,
        ],
        name="first",
    )(near, weights, covariance, first_coef, below, above, index)

    south_rows = lax.ppermute(for_up, "col", up_col)
    north_rows = lax.ppermute(for_down, "col", down_col)
    south_slab = lax.ppermute(advected, "col", up_col)
    north_slab = lax.ppermute(advected, "col", down_col)

    second_coef = slab_coef.T
    rows, picked = pl.pallas_call(
        observed_body,
        out_shape=[shape(PER_SLAB, ROWS + BLOCK), shape(BANDS, LONS, PER_BAND)],
        in_specs=[vmem()] * 6,
        out_specs=[vmem()] * 2,
        name="observed",
    )(weights, second_coef, own, north_rows, south_rows, index)

    three, two, three_blocks, two_blocks = pl.pallas_call(
        triple_body,
        out_shape=[shape(18, ROWS), shape(12, ROWS), shape(18, BLOCK), shape(12, BLOCK)],
        in_specs=[vmem()] * 3,
        out_specs=[vmem()] * 4,
        name="triple",
    )(rows, along(rows, (0, -1, 0)), along(rows, (0, 1, 0)))
    picked_all = to_all(picked, "band")
    block = pl.pallas_call(
        sort_body,
        out_shape=shape(BANDS * 8, 48, PER_BAND),
        in_specs=[vmem()] * 3,
        out_specs=vmem(),
        name="sort",
    )(three_blocks, along(three_blocks, (0, -3, 0)), along(two_blocks, (0, 3, 0)))
    line = pl.pallas_call(
        stack_body,
        out_shape=shape(48, ROWS),
        in_specs=[vmem()] * 3,
        out_specs=vmem(),
        name="stack",
    )(three, along(three, (0, -3, 0)), along(two, (0, 3, 0)))
    blocks = to_all(
        block,
        ("band", "col"),
        [
            [
                b * SLABS + x * 16 + z * 2 + k
                for b in range(BANDS)
                for x in range(4)
                for k in range(2)
            ]
            for z in range(8)
        ],
    )
    pieces = [line, beside(line, 1), beside(line, -1)]
    pieces.append(beside(pieces[1], 1))
    pieces += [along(piece, (0, 0, 1)) for piece in pieces]

    inverse = pl.pallas_call(
        inverse_first_body,
        out_shape=shape(OBS, OBS),
        in_specs=[vmem()] * 2,
        out_specs=vmem(),
        name="inverse_0",
    )(blocks, noise)
    for step in (1, 2):
        inverse = pl.pallas_call(
            partial(inverse_body, step * BLOCK),
            out_shape=shape(OBS, OBS),
            in_specs=[vmem()],
            out_specs=vmem(),
        )(inverse)

    order = pl.pallas_call(
        order_body,
        out_shape=shape(OBS, OBS),
        out_specs=vmem(),
        name="order",
    )()
    chunk = lambda height: pl.BlockSpec((height, CHUNK), lambda i: (0, i))
    return pl.pallas_call(
        update_body,
        out_shape=shape(LONS, ROWS),
        grid=(ROWS // CHUNK,),
        in_specs=[
            pl.BlockSpec((BANDS, LONS, PER_BAND), lambda i: (0, 0, 0)),
            pl.BlockSpec((OBS, OBS), lambda i: (0, 0)),
            pl.BlockSpec((OBS, OBS), lambda i: (0, 0)),
            pl.BlockSpec((LONS, 8), lambda i: (0, 0)),
        ]
        + [chunk(LONS)] * 3
        + [chunk(48)] * 8,
        out_specs=chunk(LONS),
        scratch_shapes=[pltpu.VMEM((LONS, OBS), F32), pltpu.VMEM((LONS, OBS), F32)],
        name="update",
    )(picked_all, inverse, order, second_coef, advected, north_slab, south_slab, *pieces)


def solution(mesh):
    return jax.shard_map(
        local,
        mesh=mesh,
        in_specs=(P("col", "band"), P(), P(), P(), P(), P()),
        out_specs=P("col", "band"),
        check_vma=False,
    )
```
